512 devices in a mesh: grp: 2 (over y_hi), az: 16 (over x, y_lo, core), ax: 16 (over z).
Axes of the slice: x: 4, y: 4 (y_hi: 2, y_lo: 2; y = y_hi * 2 + y_lo), z: 16, core: 2. Of those that a mesh axis runs over, the one named last changes fastest.
Arguments:
- populations: float32 [2, 27, 2, 512, 2048], P('grp', None, None, 'az', 'ax'), may hold values from 0.4 to 1.6
- relax_rates: float32 [2, 27], replicated, may hold values from 1 to 1.7
- tile_offsets: int32 [16, 16], P('ax'), may hold values from 0 to 15, each once within a row
Outputs:
- populations_next: float32 [2, 27, 2, 512, 2048], P('grp', None, None, 'az', 'ax')
The draws below stay inside these ranges and needn't reach their ends.
Inputs may be any that keep to these rules, and one draw needn't show every extreme that they name: `tile_offsets`: each row is a permutation of the 16 block offsets.
All inputs are finite; a program needn't handle non-finite values.
Results may differ from the reference program's by a relative error of at most 0.0003.
Values sent between devices are 32-bit elements; how exact they have to be, the bound alone decides.
No kernel may reach another device: no remote copies, remote signals or barrier semaphores. Data moves between devices by JAX's collectives and lax.ppermute only.
A program may use at most 64 MiB of HBM per device.

```python
import jax
import jax.numpy as jnp
from jax import lax

RADIAL = 2
AXIAL = 128
SLOTS = 2
AROUND = 512
LENGTH = 2048
N_AZ = 16
N_AX = 16


def block_scale(own_key, shape, pieces, low, largest):
    level, own = 1.0, jax.random.fold_in(own_key, 6)
    for position, parts in pieces:
        draws = jnp.exp(jax.random.uniform(jax.random.fold_in(own, position), (parts,), jnp.float32, low / len(pieces), largest / len(pieces)))
        level = level * jnp.repeat(draws, shape[position] // parts).reshape([-1 if axis == position else 1 for axis in range(len(shape))])
    return level


def setup_inputs(seed: int = 0) -> dict:
    key_of = jax.random.split(jax.random.key(seed), 4)
    return {
        "populations": jnp.clip(0.4 + 1.2 * jax.random.uniform(key_of[0], (2, 27, RADIAL, AROUND, LENGTH), jnp.float32) ** block_scale(key_of[0], (2, 27, RADIAL, AROUND, LENGTH), ((0, 2), (3, 16), (4, 16)), -0.2, 0.2), 0.4, 1.6),
        "relax_rates": jnp.clip(jax.random.uniform(key_of[1], (2, 27), jnp.float32, 1.0, 1.7), 1.0, 1.7),
        "tile_offsets": jax.vmap(lambda own: jax.random.permutation(own, N_AZ))(jax.random.split(key_of[2], N_AX)).reshape((N_AX, N_AZ)).astype(jnp.int32),
    }


exact_mode = lax.Precision.HIGHEST


def single_weight(value):
    return 2.0 / 3.0 if value == 0 else 1.0 / 6.0


def lattice_tables():
    speeds = [(radial, around, along) for radial in (-1, 0, 1) for around in (-1, 0, 1) for along in (-1, 0, 1)]
    weights = [single_weight(vector[0]) * single_weight(vector[1]) * single_weight(vector[2]) for vector in speeds]
    powers = [(first, second, third) for first in range(3) for second in range(3) for third in range(3)]
    moments = [[float(vector[0] ** power[0] * vector[1] ** power[1] * vector[2] ** power[2]) for vector in speeds] for power in powers]
    inverse_one = {-1: (0.0, -0.5, 0.5), 0: (1.0, 0.0, -1.0), 1: (0.0, 0.5, 0.5)}
    inverse = [[inverse_one[vector[0]][power[0]] * inverse_one[vector[1]][power[1]] * inverse_one[vector[2]][power[2]] for power in powers] for vector in speeds]
    return speeds, weights, moments, inverse


def operators(relax_rates):
    speeds, weights, moments, inverse = lattice_tables()
    keeping = [0.0 if index in (0, 1, 3, 9) else 1.0 for index in range(27)]
    left_table = jnp.asarray([[inverse[row][col] / weights[row] for col in range(27)] for row in range(27)], dtype=jnp.float32)
    right_table = jnp.asarray([[moments[row][col] * weights[col] for col in range(27)] for row in range(27)], dtype=jnp.float32)
    scaled = relax_rates.astype(jnp.float32) * jnp.asarray(keeping, dtype=jnp.float32)
    return jnp.einsum('im,gm,mj->gij', left_table, scaled, right_table, precision=exact_mode)


def equilibrium(state):
    speeds, weights, moments, inverse = lattice_tables()
    weight_table = jnp.asarray(weights, dtype=jnp.float32)
    drift_table = jnp.asarray([[float(speeds[row][col]) * weights[row] for col in range(3)] for row in range(27)], dtype=jnp.float32)
    speed_table = jnp.asarray([[float(speeds[row][col]) for col in range(3)] for row in range(27)], dtype=jnp.float32)
    density = jnp.einsum('i,i...->...', weight_table, state, precision=exact_mode)
    flow = jnp.einsum('ik,i...->k...', drift_table, state, precision=exact_mode) / density
    project = jnp.einsum('ik,k...->i...', speed_table, flow, precision=exact_mode)
    square = jnp.sum(flow * flow, axis=0)
    return density * (1.0 + 3.0 * project + 4.5 * project * project - 1.5 * square)


def relax(state, collision_matrix):
    return state - jnp.einsum('ij,j...->i...', collision_matrix, state - equilibrium(state), precision=exact_mode)


def stream(post, low_ghost, high_ghost):
    outgoing = []
    for index in range(27):
        radial_step = index // 9 - 1
        around_step = (index // 3) % 3 - 1
        along_step = index % 3 - 1
        moved = jnp.roll(post[index], (around_step, along_step), axis=(1, 2))
        if radial_step == 1:
            moved = jnp.concatenate([low_ghost[index - 18][None], moved[:-1]], axis=0)
        elif radial_step == -1:
            moved = jnp.concatenate([moved[1:], high_ghost[index][None]], axis=0)
        outgoing.append(moved)
    return jnp.stack(outgoing)


def bounced(post):
    return jnp.stack([post[26 - index, -1] for index in range(9)])


def mirrored(post):
    rows = []
    for index in range(18, 27):
        around_step = (index // 3) % 3 - 1
        along_step = index % 3 - 1
        rows.append(jnp.roll(post[index - 18, 0], (around_step, along_step), axis=(0, 1)))
    return jnp.stack(rows)


def route(values, tile_offsets, direction):
    shaped = values.reshape(9, N_AZ, N_AZ, SLOTS, N_AX, AXIAL)
    blocks = jnp.arange(N_AZ, dtype=jnp.int32)[:, None, None]
    source = jnp.remainder(blocks + direction * tile_offsets.astype(jnp.int32).T[None, :, :], N_AZ).astype(jnp.int32)
    full_index = jnp.broadcast_to(source[None, :, :, None, :, None], shaped.shape)
    picked = jnp.take_along_axis(shaped, full_index, axis=1)
    return picked.reshape(9, AROUND, LENGTH)


def reference(populations, relax_rates, tile_offsets):
    matrices = operators(relax_rates)
    rate_fine = relax_rates[0, 12]
    rate_core = relax_rates[1, 12]
    annulus_post = relax(populations[0], matrices[0])
    core_post = relax(populations[1], matrices[1])
    annulus_face = annulus_post[:, 0]
    annulus_balance = equilibrium(annulus_face)
    to_core = annulus_balance[0:9] + (2.0 * rate_fine / rate_core) * (annulus_face[0:9] - annulus_balance[0:9])
    core_face = core_post[:, -1]
    core_balance = equilibrium(core_face)
    to_annulus = core_balance[18:27] + (rate_core / (2.0 * rate_fine)) * (core_face[18:27] - core_balance[18:27])
    core_ghost = route(to_core, tile_offsets, -1)
    annulus_ghost = route(to_annulus, tile_offsets, 1)
    core_next = stream(core_post, mirrored(core_post), core_ghost)
    middle = stream(annulus_post, annulus_ghost, bounced(annulus_post))
    second = relax(middle, matrices[0])
    annulus_next = stream(second, annulus_ghost, bounced(second))
    return jnp.stack([annulus_next, core_next])
```

```python
import functools

import jax
import jax.numpy as jnp
from jax import lax
from jax.experimental import pallas as pl
from jax.experimental.pallas import tpu as pltpu
from jax.sharding import PartitionSpec as P

RADIAL, ROWS, FRAME, LANES = 2, 32, 40, 128
COUNT, SLOTS = 16, 2
SLOT_ROWS = 48
CORNERS = 45
EDGE = 36
OFFSET_LANE = 108
exact_mode = lax.Precision.HIGHEST
speeds = [(cr, ca, cx) for cr in (-1, 0, 1) for ca in (-1, 0, 1) for cx in (-1, 0, 1)]


def at(cr, ca, cx):
    return 9 * (cr + 1) + 3 * (ca + 1) + (cx + 1)


def moments(g):
    for stride in (1, 3, 9):
        out = [None] * 27
        for base in range(27):
            if base // stride % 3 == 0:
                low, mid, high = g[base], g[base + stride], g[base + 2 * stride]
                even = high + low
                out[base] = even + 4.0 * mid
                out[base + stride] = high - low
                out[base + 2 * stride] = even
        g = out
    return g


def balance_moments(m):
    third, ninth = 1.0 / 3.0, 1.0 / 9.0
    rho, jx, ja, jr = m[0], m[1], m[3], m[9]
    inverse = 1.0 / rho
    ur, ua, ux = jr * inverse, ja * inverse, jx * inverse
    rr, aa, xx = jr * ur, ja * ua, jx * ux
    rho3, rho9 = rho * third, rho * ninth
    jr3, ja3, jx3 = jr * third, ja * third, jx * third
    ra, rx, ax = jr * ua, jr * ux, ja * ux
    e = [None] * 27
    e[12], e[10], e[4] = ra, rx, ax
    e[18], e[6], e[2] = rho3 + rr, rho3 + aa, rho3 + xx
    e[21], e[19], e[15], e[11], e[5], e[7] = ja3, jx3, jr3, jr3, ja3, jx3
    e[22], e[16], e[14] = ax * third, rx * third, ra * third
    e[24], e[20], e[8] = rho9 + (rr + aa) * third, rho9 + (rr + xx) * third, rho9 + (aa + xx) * third
    e[25], e[23], e[17] = jx * ninth, ja * ninth, jr * ninth
    e[26] = rho * (1.0 / 27.0) + (rr + aa + xx) * ninth
    return e


def relax(g, rates):
    m = moments(g)
    e = balance_moments(m)
    d = [None] * 27
    for k in range(27):
        if k not in (0, 1, 3, 9):
            d[k] = (m[k] if e[k] is None else m[k] - e[k]) * (rates[k] * 0.125)
    for stride in (1, 3, 9):
        out = [None] * 27
        for base in range(27):
            if base // stride % 3 == 0:
                low, mid, high = d[base], d[base + stride], d[base + 2 * stride]
                out[base] = high if mid is None else high - mid
                out[base + stride] = -0.5 * high if low is None else 0.5 * (low - high)
                out[base + 2 * stride] = high if mid is None else high + mid
        d = out
    return [g[i] - d[i] for i in range(27)]


def rescaled(g, side, factor):
    m = moments(g)
    rho = m[0] * (1.0 / 216.0)
    inverse = 1.0 / m[0]
    ur, ua, ux = m[9] * inverse, m[3] * inverse, m[1] * inverse
    rest = 1.0 - 1.5 * (ur * ur + ua * ua + ux * ux)
    out = []
    for ca in (-1, 0, 1):
        for cx in (-1, 0, 1):
            along = side * ur
            along = along + ca * ua if ca else along
            along = along + cx * ux if cx else along
            e = rho * (rest + along * (3.0 + 4.5 * along))
            out.append(e + factor * (g[at(side, ca, cx)] - e))
    return out


def halo_entries(annulus, sense):
    out = []
    for depth, ca in ((1, sense), (1, 0), (2, sense)):
        if not annulus and (depth, ca) != (1, sense):
            continue
        for cx in (-1, 0, 1):
            out += [(at(0, ca, cx), 0, depth), (at(0, ca, cx), 1, depth)]
            out += [(at(1, ca, cx), 0, depth), (at(-1, ca, cx), 1, depth)]
    if annulus:
        out += [(at(1, ca, cx), 1, 1) for ca in (-1, 0, 1) for cx in (-1, 0, 1)]
    else:
        out += [(at(-1, sense, cx), 0, 1) for cx in (-1, 0, 1)]
    return out


def lanes_of(rows):
    return lax.broadcasted_iota(jnp.int32, (rows, LANES), 1)


def rows_of(rows, lanes=LANES):
    return lax.broadcasted_iota(jnp.int32, (rows, lanes), 0)


def group_and_place():
    return lax.axis_index("grp"), lax.axis_index("az")


def partner(place, group, offset):
    return (place + (1 - 2 * group) * offset + COUNT) & (COUNT - 1)


def pack_kernel(offsets, pops, low, high):
    lane, row = lanes_of(ROWS), rows_of(ROWS)
    column = jnp.zeros((ROWS, LANES), jnp.float32)
    for q in range(COUNT):
        column = jnp.where(row // SLOTS == q, offsets[0, q].astype(jnp.float32), column)
    column = jnp.where(lane == OFFSET_LANE, column, 0.0)
    first, last = column, column
    for j in range(54):
        tile = pops[j // 2, j % 2]
        own = lane // 2 == j
        first = jnp.where(own, pltpu.roll(tile, 2 * j, 1) if j else tile, first)
        last = jnp.where(own, pltpu.roll(tile, 2 * j + 2, 1), last)
    low[...] = first
    high[...] = last


def collide_kernel(rates, pops, post):
    group, _ = group_and_place()

    def chunk(step, carry):
        r, rows = step // 4, pl.ds(pl.multiple_of(step % 4 * 8, 8), 8)
        g = [pops[i, r, rows, :] for i in range(27)]
        for i, value in enumerate(relax(g, [rates[group, k] for k in range(27)])):
            post[i, r, rows, :] = value
        return carry

    lax.fori_loop(0, 8, chunk, 0)


def fill_kernel(offsets, rates, post, below, above, strips, slots, face):
    group, place = group_and_place()
    lane = lanes_of(ROWS)
    for j in range(54):
        up = pltpu.roll(above[...], (-2 * j) % LANES, 1) if j else above[...]
        down = pltpu.roll(below[...], (126 - 2 * j) % LANES, 1)
        strips[j // 2, j % 2] = jnp.where(lane < 64, up, down)

    def chunk(step, carry):
        r, rows = step // 4, pl.ds(pl.multiple_of(step % 4 * 8, 8), 8)
        g = [strips[i, r, rows, :] for i in range(27)]
        for i, value in enumerate(relax(g, [rates[group, k] for k in range(27)])):
            strips[i, r, rows, :] = value
        return carry

    lax.fori_loop(0, 8, chunk, 0)
    fine, coarse = rates[0, 12], rates[1, 12]

    def faces(source, tile, r, side, factor):
        def chunk(step, carry):
            rows = pl.ds(pl.multiple_of(step * 8, 8), 8)
            g = [source[i, r, rows, :] for i in range(27)]
            for i, value in enumerate(rescaled(g, side, factor)):
                face[i, tile, rows, :] = value
            return carry

        lax.fori_loop(0, 4, chunk, 0)

    other = COUNT * (1 - group)
    own = COUNT * group

    def halos(annulus):
        for sense in (1, -1):
            slot = own + ((place + sense + COUNT) & (COUNT - 1))
            corners = [jnp.zeros((1, LANES), jnp.float32)] * 2
            narrow = lax.broadcasted_iota(jnp.int32, (1, LANES), 1)
            for n, (i, r, depth) in enumerate(halo_entries(annulus, sense)):
                row = ROWS - depth if sense == 1 else depth - 1
                slots[slot, n : n + 1, :] = post[i, r, row : row + 1, :]
                turned = pltpu.roll(strips[i, r, row : row + 1, :], 4 * (n % 32) + 2, 1)
                corners[n // 32] = jnp.where(narrow // 4 == n % 32, turned, corners[n // 32])
            for k in range(2):
                slots[slot, CORNERS + k : CORNERS + k + 1, :] = corners[k]

    @pl.when(group == 0)
    def _():
        halos(True)
        faces(post, 0, 0, -1, 2.0 * fine / coarse)

    @pl.when(group == 1)
    def _():
        halos(False)
        faces(post, 0, 1, 1, coarse / (2.0 * fine))
        faces(strips, 1, 1, 1, coarse / (2.0 * fine))

    for q in range(COUNT):
        slot = other + partner(place, group, offsets[0, q])
        for i in range(9):
            slots[slot, 2 * i : 2 * i + 2, :] = face[i, 0, 2 * q : 2 * q + 2, :]

    @pl.when(group == 1)
    def _():
        after = other + ((place - offsets[0, COUNT - 1] + 1 + COUNT) & (COUNT - 1))
        before = other + ((place - offsets[0, 0] - 1 + COUNT) & (COUNT - 1))
        for i in range(9):
            slots[after, 18 + i : 19 + i, :] = face[i, 0, ROWS - 1 : ROWS, :]
            slots[before, 27 + i : 28 + i, :] = face[i, 0, 0:1, :]
        wide, row = lanes_of(ROWS), rows_of(ROWS)
        kind, receiver = wide // COUNT, wide % COUNT
        shift = jnp.where(kind == 2, 1, jnp.where(kind == 3, -1, 0))
        fits = ((kind < 2) & (row % 2 == kind)) | ((kind == 2) & (row == ROWS - 1)) | ((kind == 3) & (row == 0))
        picks, values = [], []
        for message, first, turn in ((below, 0, 1), (above, 9, 0)):
            offset = jnp.broadcast_to(message[:, OFFSET_LANE : OFFSET_LANE + 1], (ROWS, LANES)).astype(jnp.int32)
            target = (place - offset + shift + 2 * COUNT) & (COUNT - 1)
            picks.append(jnp.where(fits & (receiver == target), 1.0, 0.0))
            packed = jnp.zeros((ROWS, LANES), jnp.float32)
            for i in range(9):
                packed = jnp.where(wide == first + i, pltpu.roll(face[i, 1], first + i + turn, 1) if first + i + turn else face[i, 1], packed)
            values.append(packed)
        sent = lax.dot_general(
            jnp.concatenate(picks, 0),
            jnp.concatenate(values, 0),
            (((0,), (0,)), ((), ())),
            precision=exact_mode,
            preferred_element_type=jnp.float32,
        )
        line = sent[0:COUNT]
        for k in range(1, 4):
            line = line + pltpu.roll(sent[COUNT * k : COUNT * (k + 1)], 32 * k, 1)
        for e in range(COUNT):
            slots[other + e, EDGE : EDGE + 1, :] = line[e : e + 1]


def shifted(main, strip, ca, cx, lane):
    if ca:
        main, strip = pltpu.roll(main, ca % FRAME, 0), pltpu.roll(strip, ca % FRAME, 0)
    if cx:
        turned, around = pltpu.roll(main, cx % LANES, 1), pltpu.roll(strip, cx % LANES, 1)
        edge = lane == (0 if cx == 1 else LANES - 1)
        main, strip = jnp.where(edge, around, turned), jnp.where(edge, turned, around)
    return main, strip


def finish_kernel(offsets, rates, post, strips, slots, below, above, out, halo, ghost, mid):
    group, place = group_and_place()
    other = COUNT * (1 - group)
    own = COUNT * group
    lane = lanes_of(FRAME)

    def halos(annulus):
        for sense in (1, -1):
            slot = own + ((place - sense + COUNT) & (COUNT - 1))
            for n, (i, r, depth) in enumerate(halo_entries(annulus, sense)):
                row = 8 - depth if sense == 1 else depth - 1
                halo[i, r, 0, row : row + 1, :] = slots[slot, n : n + 1, :]
                line = CORNERS + n // 32
                turned = pltpu.roll(slots[slot, line : line + 1, :], (-4 * (n % 32) - 2) % LANES, 1)
                halo[i, r, 1, row : row + 1, :] = turned

    for q in range(COUNT):
        slot = other + partner(place, group, offsets[0, q])
        for i in range(9):
            ghost[i, 0, 2 * q : 2 * q + 2, :] = slots[slot, 2 * i : 2 * i + 2, :]

    def framed(i, r):
        main = jnp.concatenate([post[i, r], halo[i, r, 0]], 0)
        strip = jnp.concatenate([strips[i, r], halo[i, r, 1]], 0)
        return main, strip

    @pl.when(group == 1)
    def _():
        halos(False)
        for i, (cr, ca, cx) in enumerate(speeds):
            for r in range(RADIAL):
                source = (i, r - cr)
                if r - cr == -1:
                    source = (i - 18, 0)
                if r - cr == RADIAL:
                    out[i, r] = ghost[i, 0, 0:ROWS]
                else:
                    out[i, r] = shifted(*framed(*source), ca, cx, lane)[0][0:ROWS]

    @pl.when(group == 0)
    def _():
        halos(True)
        before = other + ((place - 1 + offsets[0, COUNT - 1] + COUNT) & (COUNT - 1))
        after = other + ((place + 1 + offsets[0, 0] + COUNT) & (COUNT - 1))
        for i in range(9):
            ghost[i, 0, FRAME - 1 : FRAME, :] = slots[before, 18 + i : 19 + i, :]
            ghost[i, 0, ROWS : ROWS + 1, :] = slots[after, 27 + i : 28 + i, :]
        received = jnp.concatenate([slots[other + d, EDGE : EDGE + 1, :] for d in range(COUNT)], 0)
        stack = jnp.concatenate([received] + [pltpu.roll(received, LANES - 32 * k, 1) for k in range(1, 4)], 0)
        row, wide = rows_of(FRAME, 64), lax.broadcasted_iota(jnp.int32, (FRAME, 64), 1)
        kind, sender = wide // COUNT, wide % COUNT
        shift = jnp.where(kind == 2, -1, jnp.where(kind == 3, 1, 0))
        fits = ((kind < 2) & (row % 2 == kind) & (row < ROWS)) | ((kind == 2) & (row == FRAME - 1)) | ((kind == 3) & (row == ROWS))
        picked = []
        for message in (below, above):
            offset = jnp.broadcast_to(message[:, OFFSET_LANE : OFFSET_LANE + 1], (ROWS, 64))
            tail = jnp.where(rows_of(8, 64) == 0, offset[0:1], offset[ROWS - 1 : ROWS])
            offset = jnp.concatenate([offset, tail], 0).astype(jnp.int32)
            source = (place + offset + shift + COUNT) & (COUNT - 1)
            pick = jnp.where(fits & (sender == source), 1.0, 0.0)
            picked.append(
                lax.dot_general(
                    pick, stack, (((1,), (0,)), ((), ())), precision=exact_mode, preferred_element_type=jnp.float32
                )
            )
        for i in range(9):
            left = pltpu.roll(picked[0], LANES - 1 - i, 1)
            right = pltpu.roll(picked[1], LANES - 9 - i, 1)
            ghost[i, 1] = jnp.where(lane < 64, right, left)

        for i, (cr, ca, cx) in enumerate(speeds):
            for r in range(RADIAL):
                if r - cr == -1:
                    main, strip = ghost[i - 18, 0], ghost[i - 18, 1]
                elif r - cr == RADIAL:
                    main, strip = framed(26 - i, 1)
                else:
                    main, strip = shifted(*framed(i, r - cr), ca, cx, lane)
                mid[i, r, 0] = main
                mid[i, r, 1] = strip

        def chunk(step, carry):
            r, tile, rows = step // 10, step // 5 % 2, pl.ds(pl.multiple_of(step % 5 * 8, 8), 8)
            g = [mid[i, r, tile, rows, :] for i in range(27)]
            for i, value in enumerate(relax(g, [rates[0, k] for k in range(27)])):
                mid[i, r, tile, rows, :] = value
            return carry

        lax.fori_loop(0, 20, chunk, 0)
        for i, (cr, ca, cx) in enumerate(speeds):
            for r in range(RADIAL):
                if r - cr == -1:
                    out[i, r] = ghost[i - 18, 0, 0:ROWS]
                elif r - cr == RADIAL:
                    out[i, r] = mid[26 - i, 1, 0, 0:ROWS]
                else:
                    main, strip = mid[i, r - cr, 0], mid[i, r - cr, 1]
                    out[i, r] = shifted(main, strip, ca, cx, lane)[0][0:ROWS]


def local(populations, relax_rates, tile_offsets):
    shape = functools.partial(jax.ShapeDtypeStruct, dtype=jnp.float32)
    block = (27, RADIAL, ROWS, LANES)
    params = pltpu.CompilerParams(vmem_limit_bytes=24 << 20)
    smem, vmem = pl.BlockSpec(memory_space=pltpu.SMEM), pl.BlockSpec(memory_space=pltpu.VMEM)
    state = populations[0]
    low, high = pl.pallas_call(
        pack_kernel,
        out_shape=(shape((ROWS, LANES)), shape((ROWS, LANES))),
        in_specs=[smem, vmem],
        out_specs=(vmem, vmem),
        compiler_params=params,
        name="pack",
    )(tile_offsets, state)
    size = lax.axis_size("ax")
    up = [(i, (i + 1) % size) for i in range(size)]
    below = lax.ppermute(high, "ax", up)
    above = lax.ppermute(low, "ax", [(j, i) for i, j in up])
    post = pl.pallas_call(
        collide_kernel,
        out_shape=shape(block),
        in_specs=[smem, vmem],
        out_specs=vmem,
        compiler_params=params,
        cost_estimate=pl.CostEstimate(flops=80_000_000, bytes_accessed=1_800_000, transcendentals=0),
        name="collide",
    )(relax_rates, state)
    strips, slots = pl.pallas_call(
        fill_kernel,
        out_shape=(shape(block), shape((2 * COUNT, SLOT_ROWS, LANES))),
        in_specs=[smem, smem, vmem, vmem, vmem],
        out_specs=(vmem, vmem),
        scratch_shapes=[pltpu.VMEM((9, 2, ROWS, LANES), jnp.float32)],
        compiler_params=params,
        name="fill",
    )(tile_offsets, relax_rates, post, below, above)
    slots = lax.all_to_all(slots, ("grp", "az"), split_axis=0, concat_axis=0, tiled=True)
    out = pl.pallas_call(
        finish_kernel,
        out_shape=shape(block),
        in_specs=[smem, smem, vmem, vmem, vmem, vmem, vmem],
        out_specs=vmem,
        scratch_shapes=[
            pltpu.VMEM((27, RADIAL, 2, 8, LANES), jnp.float32),
            pltpu.VMEM((9, 2, FRAME, LANES), jnp.float32),
            pltpu.VMEM((27, RADIAL, 2, FRAME, LANES), jnp.float32),
        ],
        compiler_params=params,
        name="finish",
    )(tile_offsets, relax_rates, post, strips, slots, below, above)
    return out[None]


def solution(mesh):
    in_specs = (P("grp", None, None, "az", "ax"), P(), P("ax", None))
    out_specs = P("grp", None, None, "az", "ax")
    return jax.shard_map(local, mesh=mesh, in_specs=in_specs, out_specs=out_specs, check_vma=False)
```

```python
import functools

import jax
import jax.numpy as jnp
from jax import lax
from jax.experimental import pallas as pl
from jax.experimental.pallas import tpu as pltpu
from jax.sharding import PartitionSpec as P


RADIAL, ROWS, FRAME, LANES = 2, 32, 40, 128
COUNT, SLOTS = 16, 2
SLOT_ROWS = 48
CORNERS = 45
EDGE = 36
OFFSET_LANE = 96
TILES = 7
exact_mode = lax.Precision.HIGHEST
speeds = [(cr, ca, cx) for cr in (-1, 0, 1) for ca in (-1, 0, 1) for cx in (-1, 0, 1)]


def at(cr, ca, cx):
    return 9 * (cr + 1) + 3 * (ca + 1) + (cx + 1)


def moments(g):
    for stride in (1, 3, 9):
        out = [None] * 27
        for base in range(27):
            if base // stride % 3 == 0:
                low, mid, high = g[base], g[base + stride], g[base + 2 * stride]
                even = high + low
                out[base] = even + 4.0 * mid
                out[base + stride] = high - low
                out[base + 2 * stride] = even
        g = out
    return g


def balance_moments(m):
    third, ninth = 1.0 / 3.0, 1.0 / 9.0
    rho, jx, ja, jr = m[0], m[1], m[3], m[9]
    inverse = 1.0 / rho
    ur, ua, ux = jr * inverse, ja * inverse, jx * inverse
    rr, aa, xx = jr * ur, ja * ua, jx * ux
    rho3, rho9 = rho * third, rho * ninth
    jr3, ja3, jx3 = jr * third, ja * third, jx * third
    ra, rx, ax = jr * ua, jr * ux, ja * ux
    e = [None] * 27
    e[12], e[10], e[4] = ra, rx, ax
    e[18], e[6], e[2] = rho3 + rr, rho3 + aa, rho3 + xx
    e[21], e[19], e[15], e[11], e[5], e[7] = ja3, jx3, jr3, jr3, ja3, jx3
    e[22], e[16], e[14] = ax * third, rx * third, ra * third
    e[24], e[20], e[8] = rho9 + (rr + aa) * third, rho9 + (rr + xx) * third, rho9 + (aa + xx) * third
    e[25], e[23], e[17] = jx * ninth, ja * ninth, jr * ninth
    e[26] = rho * (1.0 / 27.0) + (rr + aa + xx) * ninth
    return e


def relax(g, rates):
    m = moments(g)
    e = balance_moments(m)
    d = [None] * 27
    for k in range(27):
        if k not in (0, 1, 3, 9):
            d[k] = (m[k] if e[k] is None else m[k] - e[k]) * (rates[k] * 0.125)
    for stride in (1, 3, 9):
        out = [None] * 27
        for base in range(27):
            if base // stride % 3 == 0:
                low, mid, high = d[base], d[base + stride], d[base + 2 * stride]
                out[base] = high if mid is None else high - mid
                out[base + stride] = -0.5 * high if low is None else 0.5 * (low - high)
                out[base + 2 * stride] = high if mid is None else high + mid
        d = out
    return [g[i] - d[i] for i in range(27)]


def face_factor(rates, group):
    fine, coarse = rates[0, 12], rates[1, 12]
    return jnp.where(group == 0, 2.0 * fine / coarse, coarse / (2.0 * fine))


def rescaled(before, after, group, factor):
    m = moments(before)
    rho = m[0] * (1.0 / 216.0)
    inverse = 1.0 / m[0]
    ur, ua, ux = m[9] * inverse, m[3] * inverse, m[1] * inverse
    rest = 1.0 - 1.5 * (ur * ur + ua * ua + ux * ux)
    outward = jnp.where(group == 0, -ur, ur)
    out = []
    for ca in (-1, 0, 1):
        for cx in (-1, 0, 1):
            along = outward
            along = along + ca * ua if ca else along
            along = along + cx * ux if cx else along
            e = rho * (rest + along * (3.0 + 4.5 * along))
            out.append(e + factor * (after[len(out)] - e))
    return out


def halo_entries(annulus, sense):
    out = []
    for depth, ca in ((1, sense), (1, 0), (2, sense)):
        if not annulus and (depth, ca) != (1, sense):
            continue
        for cx in (-1, 0, 1):
            out += [(at(0, ca, cx), 0, depth), (at(0, ca, cx), 1, depth)]
            out += [(at(1, ca, cx), 0, depth), (at(-1, ca, cx), 1, depth)]
    if annulus:
        out += [(at(1, ca, cx), 1, 1) for ca in (-1, 0, 1) for cx in (-1, 0, 1)]
    else:
        out += [(at(-1, sense, cx), 0, 1) for cx in (-1, 0, 1)]
    return out


def lanes_of(rows):
    return lax.broadcasted_iota(jnp.int32, (rows, LANES), 1)


def rows_of(rows, lanes=LANES):
    return lax.broadcasted_iota(jnp.int32, (rows, lanes), 0)


def group_and_place():
    return lax.axis_index("grp"), lax.axis_index("az")


def partner(place, group, offset):
    return (place + (1 - 2 * group) * offset + COUNT) & (COUNT - 1)


def dense_lane(group, r):
    return 4 * (2 * group + r)


def into(acc, tile, lane, first, shift):
    turned = pltpu.roll(tile, shift % LANES, 1) if shift % LANES else tile
    return jnp.where(lane // 4 == first // 4, turned, acc)


def number_kernel(offsets, columns):
    lane = lanes_of(8)
    wide = lax.broadcasted_iota(jnp.int32, (8, COUNT), 1)
    line = jnp.broadcast_to(offsets[...].astype(jnp.float32), (8, COUNT))
    last = jnp.zeros((8, LANES), jnp.float32)
    for g in range(4):
        own = jnp.where(wide == 4 * g + rows_of(8, COUNT) // SLOTS, line, 0.0)
        last = jnp.where(lane == OFFSET_LANE + g, jnp.sum(own, axis=1, keepdims=True), last)
    columns[...] = last


def pack_kernel(columns, pops, message):
    lane = lanes_of(8)
    for i in range(27):
        if i % 4 == 0:
            acc = columns[...] if i == 24 else jnp.zeros((8, LANES), jnp.float32)
        for g in range(4):
            for r in range(RADIAL):
                first = 32 * (i % 4) + dense_lane(g, r)
                acc = into(acc, pops[i, r, 8 * g : 8 * g + 8, :], lane, first, first + 2)
        if i % 4 == 3 or i == 26:
            message[i // 4] = acc


def collide_kernel(offsets, rates, pops, post, slots, face):
    group, place = group_and_place()
    own, other = COUNT * group, COUNT * (1 - group)
    factor = face_factor(rates, group)

    def chunk(step, carry):
        r, rows = step // 4, pl.ds(pl.multiple_of(step % 4 * 8, 8), 8)
        g = [pops[i, r, rows, :] for i in range(27)]
        for i, value in enumerate(relax(g, [rates[group, k] for k in range(27)])):
            post[i, r, rows, :] = value
        return carry

    lax.fori_loop(0, 8, chunk, 0)
    for g in range(4):
        rows = slice(8 * g, 8 * g + 8)
        before = [pops[i, group, rows, :] for i in range(27)]
        after = [post[18 * group + i, group, rows, :] for i in range(9)]
        for i, value in enumerate(rescaled(before, after, group, factor)):
            face[i, rows, :] = value

    def halos(annulus):
        for sense in (1, -1):
            slot = own + ((place + sense + COUNT) & (COUNT - 1))
            for n, (i, r, depth) in enumerate(halo_entries(annulus, sense)):
                row = ROWS - depth if sense == 1 else depth - 1
                slots[slot, n : n + 1, :] = post[i, r, row : row + 1, :]

    @pl.when(group == 0)
    def _():
        halos(True)

    @pl.when(group == 1)
    def _():
        halos(False)

    for q in range(COUNT):
        slot = other + partner(place, group, offsets[0, q])
        for i in range(9):
            slots[slot, 2 * i : 2 * i + 2, :] = face[i, 2 * q : 2 * q + 2, :]
    after = other + ((place - offsets[0, COUNT - 1] + 1 + COUNT) & (COUNT - 1))
    before = other + ((place - offsets[0, 0] - 1 + COUNT) & (COUNT - 1))
    for i in range(9):
        slots[after, 18 + i : 19 + i, :] = face[i, ROWS - 1 : ROWS, :]
        slots[before, 27 + i : 28 + i, :] = face[i, 0:1, :]


def neighbour_offsets(message, width):
    lanes = [message[TILES - 1, :, OFFSET_LANE + g : OFFSET_LANE + g + 1] for g in range(4)]
    return jnp.concatenate([jnp.broadcast_to(x, (8, width)) for x in lanes], 0).astype(jnp.int32)


def edge_kernel(rates, below, above, given, strips, slots, dense, face):
    group, place = group_and_place()
    slots[...] = given[...]
    own, other = COUNT * group, COUNT * (1 - group)
    factor = face_factor(rates, group)
    lane = lanes_of(8)
    merged = [jnp.where(lane % 4 < 2, below[k], above[k]) for k in range(TILES)]
    pops = [pltpu.roll(merged[i // 4], LANES - 32 * (i % 4), 1) if i % 4 else merged[i // 4] for i in range(27)]
    for i, value in enumerate(relax(pops, [rates[group, k] for k in range(27)])):
        dense[i] = value

    def halos(annulus):
        narrow = lax.broadcasted_iota(jnp.int32, (1, LANES), 1)
        for sense in (1, -1):
            slot = own + ((place + sense + COUNT) & (COUNT - 1))
            corners = [jnp.zeros((1, LANES), jnp.float32)] * 2
            for n, (i, r, depth) in enumerate(halo_entries(annulus, sense)):
                g, row = (3, 8 - depth) if sense == 1 else (0, depth - 1)
                shift = 4 * (n % 32) - dense_lane(g, r)
                corners[n // 32] = into(corners[n // 32], dense[i, row : row + 1, :], narrow, 4 * (n % 32), shift)
            for k in range(2):
                slots[slot, CORNERS + k : CORNERS + k + 1, :] = corners[k]

    for i in range(27):
        for r in range(RADIAL):
            for g in range(4):
                shift = LANES - dense_lane(g, r) - 2
                strips[i, r, 8 * g : 8 * g + 8, :] = pltpu.roll(dense[i], shift, 1)

    @pl.when(group == 0)
    def _():
        halos(True)

    @pl.when(group == 1)
    def _():
        halos(False)
        after = [dense[18 + i] for i in range(9)]
        for i, value in enumerate(rescaled(pops, after, group, factor)):
            face[i] = value
        packed = []
        for g in range(4):
            part = jnp.zeros((8, LANES), jnp.float32)
            for i in range(9):
                shift = (2 * i - dense_lane(g, 1) - 1) % LANES
                part = jnp.where(lane // 2 == i, pltpu.roll(face[i], shift, 1) if shift else face[i], part)
            packed.append(part)
        packed = jnp.concatenate(packed, 0)
        wide, row = lanes_of(ROWS), rows_of(ROWS)
        kind, receiver = wide // COUNT, wide % COUNT
        shift = jnp.where(kind == 2, 1, jnp.where(kind == 3, -1, 0))
        fits = ((kind < 2) & (row % 2 == kind)) | ((kind == 2) & (row == ROWS - 1)) | ((kind == 3) & (row == 0))
        picks, values = [], []
        for message, side in ((below, 0), (above, 1)):
            target = (place - neighbour_offsets(message, LANES) + shift + 2 * COUNT) & (COUNT - 1)
            picks.append(jnp.where(fits & (receiver == target), 1.0, 0.0))
            values.append(jnp.where((wide % 2 == side) & (wide < 18), packed, 0.0))
        sent = lax.dot_general(
            jnp.concatenate(picks, 0),
            jnp.concatenate(values, 0),
            (((0,), (0,)), ((), ())),
            precision=exact_mode,
            preferred_element_type=jnp.float32,
        )
        line = sent[0:COUNT]
        for k in range(1, 4):
            line = line + pltpu.roll(sent[COUNT * k : COUNT * (k + 1)], 32 * k, 1)
        for e in range(COUNT):
            slots[other + e, EDGE : EDGE + 1, :] = line[e : e + 1]


def turned_by(tile, shift, axis):
    shift %= tile.shape[axis]
    return pltpu.roll(tile, shift, axis) if shift else tile


def finish_kernel(offsets, rates, post, strips, slots, below, above, out, halo, ghost, mid, side, thin, stage, sems):
    group, place = group_and_place()
    own, other = COUNT * group, COUNT * (1 - group)
    lane = lanes_of(FRAME)

    def halos(annulus):
        for sense in (1, -1):
            slot = own + ((place - sense + COUNT) & (COUNT - 1))
            for n, (i, r, depth) in enumerate(halo_entries(annulus, sense)):
                row = 8 - depth if sense == 1 else depth - 1
                halo[i, r, 0, row : row + 1, :] = slots[slot, n : n + 1, :]
                line = CORNERS + n // 32
                turned = pltpu.roll(slots[slot, line : line + 1, :], (-4 * (n % 32) - 2) % LANES, 1)
                halo[i, r, 1, row : row + 1, :] = turned

    for q in range(COUNT):
        slot = other + partner(place, group, offsets[0, q])
        for i in range(9):
            ghost[i, 0, 2 * q : 2 * q + 2, :] = slots[slot, 2 * i : 2 * i + 2, :]

    def main_of(i, r):
        return jnp.concatenate([post[i, r], halo[i, r, 0]], 0)

    def strip_of(i, r):
        return jnp.concatenate([strips[i, r], halo[i, r, 1]], 0)

    def edged(main, column, cx):
        return jnp.where(lane == (0 if cx == 1 else LANES - 1), column, turned_by(main, cx, 1)) if cx else main

    def send(i):
        if i % 3 == 2:
            pltpu.make_async_copy(stage.at[pl.ds(i - 2, 3)], out.at[pl.ds(i - 2, 3)], sems.at[i // 3]).start()

    @pl.when(group == 1)
    def _():
        halos(False)
        for i, (cr, ca, cx) in enumerate(speeds):
            for r in range(RADIAL):
                if r - cr == RADIAL:
                    stage[i, r] = ghost[i, 0, 0:ROWS]
                else:
                    source = (i - 18, 0) if r - cr == -1 else (i, r - cr)
                    main = edged(main_of(*source), turned_by(strip_of(*source), cx, 1) if cx else None, cx)
                    stage[i, r] = turned_by(main, ca, 0)[0:ROWS]
            send(i)

    @pl.when(group == 0)
    def _():
        halos(True)
        before = other + ((place - 1 + offsets[0, COUNT - 1] + COUNT) & (COUNT - 1))
        after = other + ((place + 1 + offsets[0, 0] + COUNT) & (COUNT - 1))
        for i in range(9):
            ghost[i, 0, FRAME - 1 : FRAME, :] = slots[before, 18 + i : 19 + i, :]
            ghost[i, 0, ROWS : ROWS + 1, :] = slots[after, 27 + i : 28 + i, :]
        received = jnp.concatenate([slots[other + d, EDGE : EDGE + 1, :] for d in range(COUNT)], 0)
        stack = jnp.concatenate([received] + [pltpu.roll(received, LANES - 32 * k, 1) for k in range(1, 4)], 0)
        row, wide = rows_of(FRAME, 64), lax.broadcasted_iota(jnp.int32, (FRAME, 64), 1)
        kind, sender = wide // COUNT, wide % COUNT
        shift = jnp.where(kind == 2, -1, jnp.where(kind == 3, 1, 0))
        fits = ((kind < 2) & (row % 2 == kind) & (row < ROWS)) | ((kind == 2) & (row == FRAME - 1)) | ((kind == 3) & (row == ROWS))
        picked = []
        for message in (below, above):
            offset = neighbour_offsets(message, 64)
            tail = jnp.where(rows_of(8, 64) == 0, offset[0:1], offset[ROWS - 1 : ROWS])
            source = (place + jnp.concatenate([offset, tail], 0) + shift + COUNT) & (COUNT - 1)
            pick = jnp.where(fits & (sender == source), 1.0, 0.0)
            picked.append(
                lax.dot_general(
                    pick, stack, (((1,), (0,)), ((), ())), precision=exact_mode, preferred_element_type=jnp.float32
                )
            )
        columns = jnp.where(lane % 2 == 0, picked[0], picked[1])
        for i in range(9):
            ghost[i, 1] = turned_by(columns, LANES - 1 - 2 * i, 1)

        narrow = lanes_of(8)
        for i, (cr, ca, cx) in enumerate(speeds):
            for r in range(RADIAL):
                if r - cr == -1:
                    main, strip = ghost[i - 18, 0], ghost[i - 18, 1]
                elif r - cr == RADIAL:
                    main, strip = main_of(26 - i, 1), strip_of(26 - i, 1)
                else:
                    main, strip = turned_by(main_of(i, r - cr), ca, 0), turned_by(strip_of(i, r - cr), ca, 0)
                    if cx:
                        near, far = turned_by(main, cx, 1), turned_by(strip, cx, 1)
                        edge = lane == (0 if cx == 1 else LANES - 1)
                        main, strip = jnp.where(edge, far, near), jnp.where(edge, near, far)
                mid[i, r] = main
                side[i, r] = strip

        @pl.when(place >= 0)
        def _():
            for i in range(27):
                dense = jnp.zeros((8, LANES), jnp.float32)
                for r in range(RADIAL):
                    for g in range(5):
                        first = dense_lane(g, r)
                        dense = into(dense, side[i, r, 8 * g : 8 * g + 8, :], narrow, first, first + 2)
                thin[i] = dense

        def chunk(step, carry):
            r, rows = step // 5, pl.ds(pl.multiple_of(step % 5 * 8, 8), 8)
            g = [mid[i, r, rows, :] for i in range(27)]
            for i, value in enumerate(relax(g, [rates[0, k] for k in range(27)])):
                mid[i, r, rows, :] = value
            return carry

        lax.fori_loop(0, 10, chunk, 0)
        for i, value in enumerate(relax([thin[i] for i in range(27)], [rates[0, k] for k in range(27)])):
            thin[i] = value
        for i, (cr, ca, cx) in enumerate(speeds):
            for r in range(RADIAL):
                if r - cr == -1:
                    stage[i, r] = ghost[i - 18, 0, 0:ROWS]
                elif r - cr == RADIAL:
                    stage[i, r] = mid[26 - i, 1, 0:ROWS]
                else:
                    column = None
                    if cx:
                        dense, turn = thin[i], -1 if cx == 1 else LANES - 3
                        column = [turned_by(dense, turn - dense_lane(g, r - cr), 1) for g in range(5)]
                        column = jnp.concatenate(column, 0)
                    stage[i, r] = turned_by(edged(mid[i, r - cr], column, cx), ca, 0)[0:ROWS]
            send(i)

    for k in range(9):
        pltpu.make_async_copy(stage.at[pl.ds(3 * k, 3)], out.at[pl.ds(3 * k, 3)], sems.at[k]).wait()


def local(populations, relax_rates, tile_offsets):
    shape = functools.partial(jax.ShapeDtypeStruct, dtype=jnp.float32)
    block = (27, RADIAL, ROWS, LANES)
    params = pltpu.CompilerParams(vmem_limit_bytes=24 << 20)
    smem, vmem, hbm = [pl.BlockSpec(memory_space=m) for m in (pltpu.SMEM, pltpu.VMEM, pltpu.HBM)]
    columns = pl.pallas_call(
        number_kernel,
        out_shape=shape((8, LANES)),
        in_specs=[vmem],
        out_specs=vmem,
        compiler_params=params,
        cost_estimate=pl.CostEstimate(flops=500_000_000, bytes_accessed=4_000_000, transcendentals=0),
        name="number",
    )(tile_offsets)
    message = pl.pallas_call(
        pack_kernel,
        out_shape=shape((TILES, 8, LANES)),
        in_specs=[vmem, vmem],
        out_specs=vmem,
        compiler_params=params,
        name="pack",
    )(columns, populations[0])
    size = lax.axis_size("ax")
    up = [(i, (i + 1) % size) for i in range(size)]
    below = lax.ppermute(message, "ax", up)
    above = lax.ppermute(message, "ax", [(j, i) for i, j in up])
    post, slots = pl.pallas_call(
        collide_kernel,
        out_shape=(shape(block), shape((2 * COUNT, SLOT_ROWS, LANES))),
        in_specs=[smem, smem, vmem],
        out_specs=(vmem, vmem),
        scratch_shapes=[pltpu.VMEM((9, ROWS, LANES), jnp.float32)],
        compiler_params=params,
        cost_estimate=pl.CostEstimate(flops=80_000_000, bytes_accessed=1_800_000, transcendentals=0),
        name="collide",
    )(tile_offsets, relax_rates, populations[0])
    strips, slots = pl.pallas_call(
        edge_kernel,
        out_shape=(shape(block), shape((2 * COUNT, SLOT_ROWS, LANES))),
        in_specs=[smem, vmem, vmem, vmem],
        out_specs=(vmem, vmem),
        scratch_shapes=[pltpu.VMEM((27, 8, LANES), jnp.float32), pltpu.VMEM((9, 8, LANES), jnp.float32)],
        compiler_params=params,
        name="edge",
    )(relax_rates, below, above, slots)
    slots = lax.all_to_all(slots, ("grp", "az"), split_axis=0, concat_axis=0, tiled=True)
    out = pl.pallas_call(
        finish_kernel,
        out_shape=shape(block),
        in_specs=[smem, smem, vmem, vmem, vmem, vmem, vmem],
        out_specs=hbm,
        scratch_shapes=[
            pltpu.VMEM((27, RADIAL, 2, 8, LANES), jnp.float32),
            pltpu.VMEM((9, 2, FRAME, LANES), jnp.float32),
            pltpu.VMEM((27, RADIAL, FRAME, LANES), jnp.float32),
            pltpu.VMEM((27, RADIAL, FRAME, LANES), jnp.float32),
            pltpu.VMEM((27, 8, LANES), jnp.float32),
            pltpu.VMEM(block, jnp.float32),
            pltpu.SemaphoreType.DMA((9,)),
        ],
        compiler_params=params,
        name="finish",
    )(tile_offsets, relax_rates, post, strips, slots, below, above)
    return out[None]


def solution(mesh):
    in_specs = (P("grp", None, None, "az", "ax"), P(), P("ax", None))
    out_specs = P("grp", None, None, "az", "ax")
    return jax.shard_map(local, mesh=mesh, in_specs=in_specs, out_specs=out_specs, check_vma=False)
```

```python
import functools

import jax
import jax.numpy as jnp
from jax import lax
from jax.experimental import pallas as pl
from jax.experimental.pallas import tpu as pltpu
from jax.sharding import PartitionSpec as P


RADIAL, ROWS, FRAME, LANES = 2, 32, 40, 128
COUNT, SLOTS = 16, 2
SLOT_ROWS = 40
SUMS = 30
CORNERS = 36
EDGE = 36
OFFSET_LANE = 96
TILES = 7
exact_mode = lax.Precision.HIGHEST
speeds = [(cr, ca, cx) for cr in (-1, 0, 1) for ca in (-1, 0, 1) for cx in (-1, 0, 1)]


def at(cr, ca, cx):
    return 9 * (cr + 1) + 3 * (ca + 1) + (cx + 1)


def moments(g):
    for stride in (1, 3, 9):
        out = [None] * 27
        for base in range(27):
            if base // stride % 3 == 0:
                low, mid, high = g[base], g[base + stride], g[base + 2 * stride]
                even = high + low
                out[base] = even + 4.0 * mid
                out[base + stride] = high - low
                out[base + 2 * stride] = even
        g = out
    return g


def balance_moments(m):
    third, ninth = 1.0 / 3.0, 1.0 / 9.0
    rho, jx, ja, jr = m[0], m[1], m[3], m[9]
    inverse = 1.0 / rho
    ur, ua, ux = jr * inverse, ja * inverse, jx * inverse
    rr, aa, xx = jr * ur, ja * ua, jx * ux
    rho3, rho9 = rho * third, rho * ninth
    jr3, ja3, jx3 = jr * third, ja * third, jx * third
    ra, rx, ax = jr * ua, jr * ux, ja * ux
    e = [None] * 27
    e[12], e[10], e[4] = ra, rx, ax
    e[18], e[6], e[2] = rho3 + rr, rho3 + aa, rho3 + xx
    e[21], e[19], e[15], e[11], e[5], e[7] = ja3, jx3, jr3, jr3, ja3, jx3
    e[22], e[16], e[14] = ax * third, rx * third, ra * third
    e[24], e[20], e[8] = rho9 + (rr + aa) * third, rho9 + (rr + xx) * third, rho9 + (aa + xx) * third
    e[25], e[23], e[17] = jx * ninth, ja * ninth, jr * ninth
    e[26] = rho * (1.0 / 27.0) + (rr + aa + xx) * ninth
    return e


def relax(g, rates):
    m = moments(g)
    e = balance_moments(m)
    d = [None] * 27
    for k in range(27):
        if k not in (0, 1, 3, 9):
            d[k] = (m[k] if e[k] is None else m[k] - e[k]) * (rates[k] * 0.125)
    for stride in (1, 3, 9):
        out = [None] * 27
        for base in range(27):
            if base // stride % 3 == 0:
                low, mid, high = d[base], d[base + stride], d[base + 2 * stride]
                out[base] = high if mid is None else high - mid
                out[base + stride] = -0.5 * high if low is None else 0.5 * (low - high)
                out[base + 2 * stride] = high if mid is None else high + mid
        d = out
    return [g[i] - d[i] for i in range(27)]


def face_factor(rates, group):
    fine, coarse = rates[0, 12], rates[1, 12]
    return jnp.where(group == 0, 2.0 * fine / coarse, coarse / (2.0 * fine))


def rescaled(before, after, group, factor):
    m = moments(before)
    rho = m[0] * (1.0 / 216.0)
    inverse = 1.0 / m[0]
    ur, ua, ux = m[9] * inverse, m[3] * inverse, m[1] * inverse
    rest = 1.0 - 1.5 * (ur * ur + ua * ua + ux * ux)
    outward = jnp.where(group == 0, -ur, ur)
    out = []
    for ca in (-1, 0, 1):
        for cx in (-1, 0, 1):
            along = outward
            along = along + ca * ua if ca else along
            along = along + cx * ux if cx else along
            e = rho * (rest + along * (3.0 + 4.5 * along))
            out.append(e + factor * (after[len(out)] - e))
    return out


def halo_entries(annulus, sense):
    out = []
    for depth in (1, 2) if annulus else (1,):
        for cx in (-1, 0, 1):
            out += [(at(0, sense, cx), 0, depth), (at(0, sense, cx), 1, depth)]
            out += [(at(1, sense, cx), 0, depth), (at(-1, sense, cx), 1, depth)]
    if annulus:
        out += [(at(1, ca, cx), 1, 1) for ca in (-1, 1) for cx in (-1, 0, 1)]
    else:
        out += [(at(-1, sense, cx), 0, 1) for cx in (-1, 0, 1)]
    return out


stand_ins = [(at(0, 0, 0), 0), (at(0, 0, 1), 0), (at(-1, 0, 0), 0), (at(0, 0, 0), 1), (at(0, 0, 1), 1), (at(1, 0, 0), 1)]


def stand_in_values(p0, q0, p1, r1, q1):
    quarter = 0.25
    along0 = (p0[2] - p0[0]) + quarter * (q0[2] - q0[0])
    still0 = p0[1] + quarter * (p0[2] + p0[0] - along0)
    inward0 = q0[1] + quarter * (q0[2] + q0[0])
    plus, minus = r1[1] + quarter * (r1[2] + r1[0]), q1[1] + quarter * (q1[2] + q1[0])
    along1 = (p1[2] - p1[0]) + quarter * ((r1[2] - r1[0]) + (q1[2] - q1[0]))
    still1 = p1[1] + quarter * (p1[2] + p1[0] - along1) + 0.5 * minus
    return [still0, along0, inward0, still1, along1, plus - minus]


def lanes_of(rows):
    return lax.broadcasted_iota(jnp.int32, (rows, LANES), 1)


def rows_of(rows, lanes=LANES):
    return lax.broadcasted_iota(jnp.int32, (rows, lanes), 0)


def group_and_place():
    return lax.axis_index("grp"), lax.axis_index("az")


def partner(place, group, offset):
    return (place + (1 - 2 * group) * offset + COUNT) & (COUNT - 1)


def dense_lane(group, r):
    return 4 * (2 * group + r)


def turned_by(tile, shift, axis):
    shift %= tile.shape[axis]
    return pltpu.roll(tile, shift, axis) if shift else tile


def into(acc, tile, lane, first, shift):
    turned = pltpu.roll(tile, shift % LANES, 1) if shift % LANES else tile
    return jnp.where(lane // 4 == first // 4, turned, acc)


def number_kernel(offsets, columns):
    lane = lanes_of(8)
    wide = lax.broadcasted_iota(jnp.int32, (8, COUNT), 1)
    line = jnp.broadcast_to(offsets[...].astype(jnp.float32), (8, COUNT))
    last = jnp.zeros((8, LANES), jnp.float32)
    for g in range(4):
        own = jnp.where(wide == 4 * g + rows_of(8, COUNT) // SLOTS, line, 0.0)
        last = jnp.where(lane == OFFSET_LANE + g, jnp.sum(own, axis=1, keepdims=True), last)
    columns[...] = last


def pack_kernel(columns, pops, message):
    lane = lanes_of(8)
    for i in range(27):
        if i % 4 == 0:
            acc = columns[...] if i == 24 else jnp.zeros((8, LANES), jnp.float32)
        for g in range(4):
            for r in range(RADIAL):
                first = 32 * (i % 4) + dense_lane(g, r)
                acc = into(acc, pops[i, r, 8 * g : 8 * g + 8, :], lane, first, first + 2)
        if i % 4 == 3 or i == 26:
            message[i // 4] = acc


def collide_kernel(offsets, rates, pops, post, slots, face):
    group, place = group_and_place()
    own, other = COUNT * group, COUNT * (1 - group)
    factor = face_factor(rates, group)

    def chunk(step, carry):
        r, rows = step // 4, pl.ds(pl.multiple_of(step % 4 * 8, 8), 8)
        g = [pops[i, r, rows, :] for i in range(27)]
        for i, value in enumerate(relax(g, [rates[group, k] for k in range(27)])):
            post[i, r, rows, :] = value
        return carry

    lax.fori_loop(0, 8, chunk, 0)
    for g in range(4):
        rows = slice(8 * g, 8 * g + 8)
        before = [pops[i, group, rows, :] for i in range(27)]
        after = [post[18 * group + i, group, rows, :] for i in range(9)]
        for i, value in enumerate(rescaled(before, after, group, factor)):
            face[i, rows, :] = value

    def halos(annulus):
        for sense in (1, -1):
            slot = own + ((place + sense + COUNT) & (COUNT - 1))
            for n, (i, r, depth) in enumerate(halo_entries(annulus, sense)):
                row = ROWS - depth if sense == 1 else depth - 1
                slots[slot, n : n + 1, :] = post[i, r, row : row + 1, :]

    @pl.when(group == 0)
    def _():
        halos(True)

    @pl.when(group == 1)
    def _():
        halos(False)

    for q in range(COUNT):
        slot = other + partner(place, group, offsets[0, q])
        for i in range(9):
            slots[slot, 2 * i : 2 * i + 2, :] = face[i, 2 * q : 2 * q + 2, :]
    after = other + ((place - offsets[0, COUNT - 1] + 1 + COUNT) & (COUNT - 1))
    before = other + ((place - offsets[0, 0] - 1 + COUNT) & (COUNT - 1))
    for i in range(9):
        slots[after, 18 + i : 19 + i, :] = face[i, ROWS - 1 : ROWS, :]
        slots[before, 27 + i : 28 + i, :] = face[i, 0:1, :]


def neighbour_offsets(message, width):
    lanes = [message[TILES - 1, :, OFFSET_LANE + g : OFFSET_LANE + g + 1] for g in range(4)]
    return jnp.concatenate([jnp.broadcast_to(x, (8, width)) for x in lanes], 0).astype(jnp.int32)


def halo_sums(post, strips, group):
    rows, lane = slice(8 * group, 8 * group + 8), lanes_of(8)

    def moved(cr, r):
        out = []
        for cx in (-1, 0, 1):
            main, strip = post[at(cr, 0, cx), r, rows, :], strips[at(cr, 0, cx), r, rows, :]
            if cx:
                near, far = turned_by(main, cx, 1), turned_by(strip, cx, 1)
                edge = lane == (0 if cx == 1 else LANES - 1)
                main, strip = jnp.where(edge, far, near), jnp.where(edge, near, far)
            out.append((main, strip))
        return out

    back = [(post[at(1, 0, -cx), 1, rows, :], strips[at(1, 0, -cx), 1, rows, :]) for cx in (-1, 0, 1)]
    parts = [moved(0, 0), moved(-1, 1), moved(0, 1), moved(1, 0), back]
    main, strip = [stand_in_values(*[[value[k] for value in part] for part in parts]) for k in (0, 1)]
    return list(zip(main, strip))


def edge_kernel(rates, post, below, above, given, strips, slots, dense, face):
    group, place = group_and_place()
    slots[...] = given[...]
    own, other = COUNT * group, COUNT * (1 - group)
    factor = face_factor(rates, group)
    lane = lanes_of(8)
    merged = [jnp.where(lane % 4 < 2, below[k], above[k]) for k in range(TILES)]
    pops = [pltpu.roll(merged[i // 4], LANES - 32 * (i % 4), 1) if i % 4 else merged[i // 4] for i in range(27)]
    for i, value in enumerate(relax(pops, [rates[group, k] for k in range(27)])):
        dense[i] = value

    def halos(annulus):
        narrow = lax.broadcasted_iota(jnp.int32, (1, LANES), 1)
        for sense in (1, -1):
            slot = own + ((place + sense + COUNT) & (COUNT - 1))
            corners = [jnp.zeros((1, LANES), jnp.float32)] * 2
            for n, (i, r, depth) in enumerate(halo_entries(annulus, sense)):
                g, row = (3, 8 - depth) if sense == 1 else (0, depth - 1)
                shift = 4 * (n % 32) - dense_lane(g, r)
                corners[n // 32] = into(corners[n // 32], dense[i, row : row + 1, :], narrow, 4 * (n % 32), shift)
            if annulus:
                row = 7 if sense == 1 else 0
                for n, (main, strip) in enumerate(halo_sums(post, strips, 3 if sense == 1 else 0), SUMS):
                    slots[slot, n : n + 1, :] = main[row : row + 1]
                    shift = (4 * (n % 32) + 2) % LANES
                    corners[n // 32] = into(corners[n // 32], strip[row : row + 1], narrow, 4 * (n % 32), shift)
            for k in range(2):
                slots[slot, CORNERS + k : CORNERS + k + 1, :] = corners[k]

    for i in range(27):
        for r in range(RADIAL):
            for g in range(4):
                shift = LANES - dense_lane(g, r) - 2
                strips[i, r, 8 * g : 8 * g + 8, :] = pltpu.roll(dense[i], shift, 1)

    @pl.when(group == 0)
    def _():
        halos(True)

    @pl.when(group == 1)
    def _():
        halos(False)
        after = [dense[18 + i] for i in range(9)]
        for i, value in enumerate(rescaled(pops, after, group, factor)):
            face[i] = value
        packed = []
        for g in range(4):
            part = jnp.zeros((8, LANES), jnp.float32)
            for i in range(9):
                shift = (2 * i - dense_lane(g, 1) - 1) % LANES
                part = jnp.where(lane // 2 == i, pltpu.roll(face[i], shift, 1) if shift else face[i], part)
            packed.append(part)
        packed = jnp.concatenate(packed, 0)
        wide, row = lanes_of(ROWS), rows_of(ROWS)
        kind, receiver = wide // COUNT, wide % COUNT
        shift = jnp.where(kind == 2, 1, jnp.where(kind == 3, -1, 0))
        fits = ((kind < 2) & (row % 2 == kind)) | ((kind == 2) & (row == ROWS - 1)) | ((kind == 3) & (row == 0))
        picks, values = [], []
        for message, side in ((below, 0), (above, 1)):
            target = (place - neighbour_offsets(message, LANES) + shift + 2 * COUNT) & (COUNT - 1)
            picks.append(jnp.where(fits & (receiver == target), 1.0, 0.0))
            values.append(jnp.where((wide % 2 == side) & (wide < 18), packed, 0.0))
        sent = lax.dot_general(
            jnp.concatenate(picks, 0),
            jnp.concatenate(values, 0),
            (((0,), (0,)), ((), ())),
            precision=exact_mode,
            preferred_element_type=jnp.float32,
        )
        line = sent[0:COUNT]
        for k in range(1, 4):
            line = line + pltpu.roll(sent[COUNT * k : COUNT * (k + 1)], 32 * k, 1)
        for e in range(COUNT):
            slots[other + e, EDGE : EDGE + 1, :] = line[e : e + 1]


def finish_kernel(offsets, rates, post, strips, slots, below, above, out, halo, stand, ghost, mid, side, thin, stage, sems):
    group, place = group_and_place()
    own, other = COUNT * group, COUNT * (1 - group)
    lane = lanes_of(FRAME)

    def halos(annulus):
        for sense in (1, -1):
            slot = own + ((place - sense + COUNT) & (COUNT - 1))
            for n, (i, r, depth) in enumerate(halo_entries(annulus, sense)):
                row = 8 - depth if sense == 1 else depth - 1
                halo[i, r, 0, row : row + 1, :] = slots[slot, n : n + 1, :]
                line = CORNERS + n // 32
                turned = pltpu.roll(slots[slot, line : line + 1, :], (-4 * (n % 32) - 2) % LANES, 1)
                halo[i, r, 1, row : row + 1, :] = turned
            if annulus:
                for n in range(SUMS, SUMS + 6):
                    row = 7 if sense == 1 else 0
                    stand[n - SUMS, 0, row : row + 1, :] = slots[slot, n : n + 1, :]
                    line = CORNERS + n // 32
                    turned = pltpu.roll(slots[slot, line : line + 1, :], (-4 * (n % 32) - 2) % LANES, 1)
                    stand[n - SUMS, 1, row : row + 1, :] = turned

    for q in range(COUNT):
        slot = other + partner(place, group, offsets[0, q])
        for i in range(9):
            ghost[i, 0, 2 * q : 2 * q + 2, :] = slots[slot, 2 * i : 2 * i + 2, :]

    def main_of(i, r):
        return jnp.concatenate([post[i, r], halo[i, r, 0]], 0)

    def strip_of(i, r):
        return jnp.concatenate([strips[i, r], halo[i, r, 1]], 0)

    def edged(main, column, cx):
        return jnp.where(lane == (0 if cx == 1 else LANES - 1), column, turned_by(main, cx, 1)) if cx else main

    def send(i):
        if i % 3 == 2:
            pltpu.make_async_copy(stage.at[pl.ds(i - 2, 3)], out.at[pl.ds(i - 2, 3)], sems.at[i // 3]).start()

    @pl.when(group == 1)
    def _():
        halos(False)
        for i, (cr, ca, cx) in enumerate(speeds):
            for r in range(RADIAL):
                if r - cr == RADIAL:
                    stage[i, r] = ghost[i, 0, 0:ROWS]
                else:
                    source = (i - 18, 0) if r - cr == -1 else (i, r - cr)
                    main = edged(main_of(*source), turned_by(strip_of(*source), cx, 1) if cx else None, cx)
                    stage[i, r] = turned_by(main, ca, 0)[0:ROWS]
            send(i)

    @pl.when(group == 0)
    def _():
        halos(True)
        before = other + ((place - 1 + offsets[0, COUNT - 1] + COUNT) & (COUNT - 1))
        after = other + ((place + 1 + offsets[0, 0] + COUNT) & (COUNT - 1))
        for i in range(9):
            ghost[i, 0, FRAME - 1 : FRAME, :] = slots[before, 18 + i : 19 + i, :]
            ghost[i, 0, ROWS : ROWS + 1, :] = slots[after, 27 + i : 28 + i, :]
        received = jnp.concatenate([slots[other + d, EDGE : EDGE + 1, :] for d in range(COUNT)], 0)
        stack = jnp.concatenate([received] + [pltpu.roll(received, LANES - 32 * k, 1) for k in range(1, 4)], 0)
        row, wide = rows_of(FRAME, 64), lax.broadcasted_iota(jnp.int32, (FRAME, 64), 1)
        kind, sender = wide // COUNT, wide % COUNT
        shift = jnp.where(kind == 2, -1, jnp.where(kind == 3, 1, 0))
        fits = ((kind < 2) & (row % 2 == kind) & (row < ROWS)) | ((kind == 2) & (row == FRAME - 1)) | ((kind == 3) & (row == ROWS))
        picked = []
        for message in (below, above):
            offset = neighbour_offsets(message, 64)
            tail = jnp.where(rows_of(8, 64) == 0, offset[0:1], offset[ROWS - 1 : ROWS])
            source = (place + jnp.concatenate([offset, tail], 0) + shift + COUNT) & (COUNT - 1)
            pick = jnp.where(fits & (sender == source), 1.0, 0.0)
            picked.append(
                lax.dot_general(
                    pick, stack, (((1,), (0,)), ((), ())), precision=exact_mode, preferred_element_type=jnp.float32
                )
            )
        columns = jnp.where(lane % 2 == 0, picked[0], picked[1])
        for i in range(9):
            ghost[i, 1] = turned_by(columns, LANES - 1 - 2 * i, 1)

        narrow, none = lanes_of(8), jnp.zeros((8, LANES), jnp.float32)
        for i, (cr, ca, cx) in enumerate(speeds):
            for r in range(RADIAL):
                if r - cr == -1:
                    main, strip = ghost[i - 18, 0], ghost[i - 18, 1]
                elif r - cr == RADIAL:
                    main, strip = main_of(26 - i, 1), strip_of(26 - i, 1)
                else:
                    main, strip = turned_by(main_of(i, r - cr), ca, 0), turned_by(strip_of(i, r - cr), ca, 0)
                    if cx:
                        near, far = turned_by(main, cx, 1), turned_by(strip, cx, 1)
                        edge = lane == (0 if cx == 1 else LANES - 1)
                        main, strip = jnp.where(edge, far, near), jnp.where(edge, near, far)
                if ca or r - cr == -1:
                    mid[i, r] = main
                    side[i, r] = strip
                else:
                    mid[i, r, 0:ROWS] = main[0:ROWS]
                    side[i, r, 0:ROWS] = strip[0:ROWS]
                    given = (i, r) in stand_ins
                    mid[i, r, ROWS:FRAME] = stand[stand_ins.index((i, r)), 0] if given else none
                    side[i, r, ROWS:FRAME] = stand[stand_ins.index((i, r)), 1] if given else none

        @pl.when(place >= 0)
        def _():
            for i in range(27):
                dense = jnp.zeros((8, LANES), jnp.float32)
                for r in range(RADIAL):
                    for g in range(5):
                        first = dense_lane(g, r)
                        dense = into(dense, side[i, r, 8 * g : 8 * g + 8, :], narrow, first, first + 2)
                thin[i] = dense

        def chunk(step, carry):
            r, rows = step // 5, pl.ds(pl.multiple_of(step % 5 * 8, 8), 8)
            g = [mid[i, r, rows, :] for i in range(27)]
            for i, value in enumerate(relax(g, [rates[0, k] for k in range(27)])):
                mid[i, r, rows, :] = value
            return carry

        lax.fori_loop(0, 10, chunk, 0)
        for i, value in enumerate(relax([thin[i] for i in range(27)], [rates[0, k] for k in range(27)])):
            thin[i] = value
        for i, (cr, ca, cx) in enumerate(speeds):
            for r in range(RADIAL):
                if r - cr == -1:
                    stage[i, r] = ghost[i - 18, 0, 0:ROWS]
                elif r - cr == RADIAL:
                    stage[i, r] = mid[26 - i, 1, 0:ROWS]
                else:
                    column = None
                    if cx:
                        dense, turn = thin[i], -1 if cx == 1 else LANES - 3
                        column = [turned_by(dense, turn - dense_lane(g, r - cr), 1) for g in range(5)]
                        column = jnp.concatenate(column, 0)
                    stage[i, r] = turned_by(edged(mid[i, r - cr], column, cx), ca, 0)[0:ROWS]
            send(i)

    for k in range(9):
        pltpu.make_async_copy(stage.at[pl.ds(3 * k, 3)], out.at[pl.ds(3 * k, 3)], sems.at[k]).wait()


def local(populations, relax_rates, tile_offsets):
    shape = functools.partial(jax.ShapeDtypeStruct, dtype=jnp.float32)
    block = (27, RADIAL, ROWS, LANES)
    params = pltpu.CompilerParams(vmem_limit_bytes=24 << 20)
    smem, vmem, hbm = [pl.BlockSpec(memory_space=m) for m in (pltpu.SMEM, pltpu.VMEM, pltpu.HBM)]
    columns = pl.pallas_call(
        number_kernel,
        out_shape=shape((8, LANES)),
        in_specs=[vmem],
        out_specs=vmem,
        compiler_params=params,
        cost_estimate=pl.CostEstimate(flops=500_000_000, bytes_accessed=4_000_000, transcendentals=0),
        name="number",
    )(tile_offsets)
    message = pl.pallas_call(
        pack_kernel,
        out_shape=shape((TILES, 8, LANES)),
        in_specs=[vmem, vmem],
        out_specs=vmem,
        compiler_params=params,
        name="pack",
    )(columns, populations[0])
    size = lax.axis_size("ax")
    up = [(i, (i + 1) % size) for i in range(size)]
    below = lax.ppermute(message, "ax", up)
    above = lax.ppermute(message, "ax", [(j, i) for i, j in up])
    post, slots = pl.pallas_call(
        collide_kernel,
        out_shape=(shape(block), shape((2 * COUNT, SLOT_ROWS, LANES))),
        in_specs=[smem, smem, vmem],
        out_specs=(vmem, vmem),
        scratch_shapes=[pltpu.VMEM((9, ROWS, LANES), jnp.float32)],
        compiler_params=params,
        cost_estimate=pl.CostEstimate(flops=80_000_000, bytes_accessed=1_800_000, transcendentals=0),
        name="collide",
    )(tile_offsets, relax_rates, populations[0])
    strips, slots = pl.pallas_call(
        edge_kernel,
        out_shape=(shape(block), shape((2 * COUNT, SLOT_ROWS, LANES))),
        in_specs=[smem, vmem, vmem, vmem, vmem],
        out_specs=(vmem, vmem),
        scratch_shapes=[pltpu.VMEM((27, 8, LANES), jnp.float32), pltpu.VMEM((9, 8, LANES), jnp.float32)],
        compiler_params=params,
        name="edge",
    )(relax_rates, post, below, above, slots)
    slots = lax.all_to_all(slots, ("grp", "az"), split_axis=0, concat_axis=0, tiled=True)
    out = pl.pallas_call(
        finish_kernel,
        out_shape=shape(block),
        in_specs=[smem, smem, vmem, vmem, vmem, vmem, vmem],
        out_specs=hbm,
        scratch_shapes=[
            pltpu.VMEM((27, RADIAL, 2, 8, LANES), jnp.float32),
            pltpu.VMEM((6, 2, 8, LANES), jnp.float32),
            pltpu.VMEM((9, 2, FRAME, LANES), jnp.float32),
            pltpu.VMEM((27, RADIAL, FRAME, LANES), jnp.float32),
            pltpu.VMEM((27, RADIAL, FRAME, LANES), jnp.float32),
            pltpu.VMEM((27, 8, LANES), jnp.float32),
            pltpu.VMEM(block, jnp.float32),
            pltpu.SemaphoreType.DMA((9,)),
        ],
        compiler_params=params,
        name="finish",
    )(tile_offsets, relax_rates, post, strips, slots, below, above)
    return out[None]


def solution(mesh):
    in_specs = (P("grp", None, None, "az", "ax"), P(), P("ax", None))
    out_specs = P("grp", None, None, "az", "ax")
    return jax.shard_map(local, mesh=mesh, in_specs=in_specs, out_specs=out_specs, check_vma=False)
```

```python
import functools

import jax
import jax.numpy as jnp
from jax import lax
from jax.experimental import pallas as pl
from jax.experimental.pallas import tpu as pltpu
from jax.sharding import PartitionSpec as P


RADIAL, ROWS, FRAME, LANES = 2, 32, 40, 128
COUNT, SLOTS = 16, 2
SLOT_ROWS = 40
SUMS = 30
CORNERS = 36
EDGE = 36
OFFSET_LANE = 96
TILES = 7
exact_mode = lax.Precision.HIGHEST
speeds = [(cr, ca, cx) for cr in (-1, 0, 1) for ca in (-1, 0, 1) for cx in (-1, 0, 1)]


def at(cr, ca, cx):
    return 9 * (cr + 1) + 3 * (ca + 1) + (cx + 1)


def moments(g):
    for stride in (1, 3, 9):
        out = [None] * 27
        for base in range(27):
            if base // stride % 3 == 0:
                low, mid, high = g[base], g[base + stride], g[base + 2 * stride]
                even = high + low
                out[base] = even + 4.0 * mid
                out[base + stride] = high - low
                out[base + 2 * stride] = even
        g = out
    return g


def balance_moments(m):
    third, ninth = 1.0 / 3.0, 1.0 / 9.0
    rho, jx, ja, jr = m[0], m[1], m[3], m[9]
    inverse = 1.0 / rho
    ur, ua, ux = jr * inverse, ja * inverse, jx * inverse
    rr, aa, xx = jr * ur, ja * ua, jx * ux
    rho3, rho9 = rho * third, rho * ninth
    jr3, ja3, jx3 = jr * third, ja * third, jx * third
    ra, rx, ax = jr * ua, jr * ux, ja * ux
    e = [None] * 27
    e[12], e[10], e[4] = ra, rx, ax
    e[18], e[6], e[2] = rho3 + rr, rho3 + aa, rho3 + xx
    e[21], e[19], e[15], e[11], e[5], e[7] = ja3, jx3, jr3, jr3, ja3, jx3
    e[22], e[16], e[14] = ax * third, rx * third, ra * third
    e[24], e[20], e[8] = rho9 + (rr + aa) * third, rho9 + (rr + xx) * third, rho9 + (aa + xx) * third
    e[25], e[23], e[17] = jx * ninth, ja * ninth, jr * ninth
    e[26] = rho * (1.0 / 27.0) + (rr + aa + xx) * ninth
    return e


def relax(g, rates):
    m = moments(g)
    e = balance_moments(m)
    d = [None] * 27
    for k in range(27):
        if k not in (0, 1, 3, 9):
            d[k] = (m[k] if e[k] is None else m[k] - e[k]) * rates[k]
    for stride in (1, 3, 9):
        out = [None] * 27
        for base in range(27):
            if base // stride % 3 == 0:
                low, mid, high = d[base], d[base + stride], d[base + 2 * stride]
                out[base] = high if mid is None else high - mid
                out[base + stride] = -0.5 * high if low is None else 0.5 * (low - high)
                out[base + 2 * stride] = high if mid is None else high + mid
        d = out
    return [g[i] - d[i] for i in range(27)]


def face_factor(rates, group):
    fine, coarse = rates[0, 12], rates[1, 12]
    return jnp.where(group == 0, 2.0 * fine / coarse, coarse / (2.0 * fine))


def rescaled(before, after, group, factor):
    m = moments(before)
    rho = m[0] * (1.0 / 216.0)
    inverse = 1.0 / m[0]
    ur, ua, ux = m[9] * inverse, m[3] * inverse, m[1] * inverse
    rest = 1.0 - 1.5 * (ur * ur + ua * ua + ux * ux)
    outward = jnp.where(group == 0, -ur, ur)
    out = []
    for ca in (-1, 0, 1):
        for cx in (-1, 0, 1):
            along = outward
            along = along + ca * ua if ca else along
            along = along + cx * ux if cx else along
            e = rho * (rest + along * (3.0 + 4.5 * along))
            out.append(e + factor * (after[len(out)] - e))
    return out


def halo_entries(annulus, sense):
    out = []
    for depth in (1, 2) if annulus else (1,):
        for cx in (-1, 0, 1):
            out += [(at(0, sense, cx), 0, depth), (at(0, sense, cx), 1, depth)]
            out += [(at(1, sense, cx), 0, depth), (at(-1, sense, cx), 1, depth)]
    if annulus:
        out += [(at(1, ca, cx), 1, 1) for ca in (-1, 1) for cx in (-1, 0, 1)]
    else:
        out += [(at(-1, sense, cx), 0, 1) for cx in (-1, 0, 1)]
    return out


stand_ins = [(at(0, 0, 0), 0), (at(0, 0, 1), 0), (at(-1, 0, 0), 0), (at(0, 0, 0), 1), (at(0, 0, 1), 1), (at(1, 0, 0), 1)]


def stand_in_values(p0, q0, p1, r1, q1):
    quarter = 0.25
    along0 = (p0[2] - p0[0]) + quarter * (q0[2] - q0[0])
    still0 = p0[1] + quarter * (p0[2] + p0[0] - along0)
    inward0 = q0[1] + quarter * (q0[2] + q0[0])
    plus, minus = r1[1] + quarter * (r1[2] + r1[0]), q1[1] + quarter * (q1[2] + q1[0])
    along1 = (p1[2] - p1[0]) + quarter * ((r1[2] - r1[0]) + (q1[2] - q1[0]))
    still1 = p1[1] + quarter * (p1[2] + p1[0] - along1) + 0.5 * minus
    return [still0, along0, inward0, still1, along1, plus - minus]


def lanes_of(rows):
    return lax.broadcasted_iota(jnp.int32, (rows, LANES), 1)


def rows_of(rows, lanes=LANES):
    return lax.broadcasted_iota(jnp.int32, (rows, lanes), 0)


def group_and_place():
    return lax.axis_index("grp"), lax.axis_index("az")


def partner(place, group, offset):
    return (place + (1 - 2 * group) * offset + COUNT) & (COUNT - 1)


def dense_lane(group, r):
    return 4 * (2 * group + r)


def turned_by(tile, shift, axis):
    shift %= tile.shape[axis]
    return pltpu.roll(tile, shift, axis) if shift else tile


def into(acc, tile, lane, first, shift):
    turned = pltpu.roll(tile, shift % LANES, 1) if shift % LANES else tile
    return jnp.where(lane // 4 == first // 4, turned, acc)


def number_kernel(offsets, columns):
    lane = lanes_of(8)
    wide = lax.broadcasted_iota(jnp.int32, (8, COUNT), 1)
    line = jnp.broadcast_to(offsets[...].astype(jnp.float32), (8, COUNT))
    last = jnp.zeros((8, LANES), jnp.float32)
    for g in range(4):
        own = jnp.where(wide == 4 * g + rows_of(8, COUNT) // SLOTS, line, 0.0)
        last = jnp.where(lane == OFFSET_LANE + g, jnp.sum(own, axis=1, keepdims=True), last)
    columns[...] = last


def pack_kernel(columns, pops, message):
    lane = lanes_of(8)
    for i in range(27):
        if i % 4 == 0:
            acc = columns[...] if i == 24 else jnp.zeros((8, LANES), jnp.float32)
        for g in range(4):
            for r in range(RADIAL):
                first = 32 * (i % 4) + dense_lane(g, r)
                acc = into(acc, pops[i, r, 8 * g : 8 * g + 8, :], lane, first, first + 2)
        if i % 4 == 3 or i == 26:
            message[i // 4] = acc


def collide_kernel(offsets, rates, pops, post, slots, scales, face):
    group, place = group_and_place()
    own, other = COUNT * group, COUNT * (1 - group)
    factor = face_factor(rates, group)
    scaled = [rates[group, k] * 0.125 for k in range(27)]
    for k, value in enumerate(scaled + [factor]):
        scales[k] = jnp.full((8, LANES), value, jnp.float32)

    def chunk(step, carry):
        r, rows = step // 4, pl.ds(pl.multiple_of(step % 4 * 8, 8), 8)
        g = [pops[i, r, rows, :] for i in range(27)]
        for i, value in enumerate(relax(g, scaled)):
            post[i, r, rows, :] = value
        return carry

    lax.fori_loop(0, 8, chunk, 0)
    for g in range(4):
        rows = slice(8 * g, 8 * g + 8)
        before = [pops[i, group, rows, :] for i in range(27)]
        after = [post[18 * group + i, group, rows, :] for i in range(9)]
        for i, value in enumerate(rescaled(before, after, group, factor)):
            face[i, rows, :] = value

    def halos(annulus):
        for sense in (1, -1):
            slot = own + ((place + sense + COUNT) & (COUNT - 1))
            for n, (i, r, depth) in enumerate(halo_entries(annulus, sense)):
                row = ROWS - depth if sense == 1 else depth - 1
                slots[slot, n : n + 1, :] = post[i, r, row : row + 1, :]

    @pl.when(group == 0)
    def _():
        halos(True)

    @pl.when(group == 1)
    def _():
        halos(False)

    for q in range(COUNT):
        slot = other + partner(place, group, offsets[0, q])
        for i in range(9):
            slots[slot, 2 * i : 2 * i + 2, :] = face[i, 2 * q : 2 * q + 2, :]
    after = other + ((place - offsets[0, COUNT - 1] + 1 + COUNT) & (COUNT - 1))
    before = other + ((place - offsets[0, 0] - 1 + COUNT) & (COUNT - 1))
    for i in range(9):
        slots[after, 18 + i : 19 + i, :] = face[i, ROWS - 1 : ROWS, :]
        slots[before, 27 + i : 28 + i, :] = face[i, 0:1, :]


def neighbour_offsets(message, width):
    lanes = [message[TILES - 1, :, OFFSET_LANE + g : OFFSET_LANE + g + 1] for g in range(4)]
    return jnp.concatenate([jnp.broadcast_to(x, (8, width)) for x in lanes], 0).astype(jnp.int32)


def halo_sums(post, strips, group):
    rows, lane = slice(8 * group, 8 * group + 8), lanes_of(8)

    def moved(cr, r):
        out = []
        for cx in (-1, 0, 1):
            main, strip = post[at(cr, 0, cx), r, rows, :], strips[at(cr, 0, cx), r, rows, :]
            if cx:
                near, far = turned_by(main, cx, 1), turned_by(strip, cx, 1)
                edge = lane == (0 if cx == 1 else LANES - 1)
                main, strip = jnp.where(edge, far, near), jnp.where(edge, near, far)
            out.append((main, strip))
        return out

    back = [(post[at(1, 0, -cx), 1, rows, :], strips[at(1, 0, -cx), 1, rows, :]) for cx in (-1, 0, 1)]
    parts = [moved(0, 0), moved(-1, 1), moved(0, 1), moved(1, 0), back]
    main, strip = [stand_in_values(*[[value[k] for value in part] for part in parts]) for k in (0, 1)]
    return list(zip(main, strip))


def edge_kernel(scales, post, below, above, given, strips, slots, dense, face):
    group, place = group_and_place()
    slots[...] = given[...]
    own, other = COUNT * group, COUNT * (1 - group)
    factor = scales[27]
    lane = lanes_of(8)
    merged = [jnp.where(lane % 4 < 2, below[k], above[k]) for k in range(TILES)]
    pops = [pltpu.roll(merged[i // 4], LANES - 32 * (i % 4), 1) if i % 4 else merged[i // 4] for i in range(27)]
    for i, value in enumerate(relax(pops, [scales[k] for k in range(27)])):
        dense[i] = value

    def halos(annulus):
        narrow = lax.broadcasted_iota(jnp.int32, (1, LANES), 1)
        for sense in (1, -1):
            slot = own + ((place + sense + COUNT) & (COUNT - 1))
            corners = [jnp.zeros((1, LANES), jnp.float32)] * 2
            for n, (i, r, depth) in enumerate(halo_entries(annulus, sense)):
                g, row = (3, 8 - depth) if sense == 1 else (0, depth - 1)
                shift = 4 * (n % 32) - dense_lane(g, r)
                corners[n // 32] = into(corners[n // 32], dense[i, row : row + 1, :], narrow, 4 * (n % 32), shift)
            if annulus:
                row = 7 if sense == 1 else 0
                for n, (main, strip) in enumerate(halo_sums(post, strips, 3 if sense == 1 else 0), SUMS):
                    slots[slot, n : n + 1, :] = main[row : row + 1]
                    shift = (4 * (n % 32) + 2) % LANES
                    corners[n // 32] = into(corners[n // 32], strip[row : row + 1], narrow, 4 * (n % 32), shift)
            for k in range(2):
                slots[slot, CORNERS + k : CORNERS + k + 1, :] = corners[k]

    for i in range(27):
        for r in range(RADIAL):
            for g in range(4):
                shift = LANES - dense_lane(g, r) - 2
                strips[i, r, 8 * g : 8 * g + 8, :] = pltpu.roll(dense[i], shift, 1)

    @pl.when(group == 0)
    def _():
        halos(True)

    @pl.when(group == 1)
    def _():
        halos(False)
        after = [dense[18 + i] for i in range(9)]
        for i, value in enumerate(rescaled(pops, after, group, factor)):
            face[i] = value
        packed = []
        for g in range(4):
            part = jnp.zeros((8, LANES), jnp.float32)
            for i in range(9):
                shift = (2 * i - dense_lane(g, 1) - 1) % LANES
                part = jnp.where(lane // 2 == i, pltpu.roll(face[i], shift, 1) if shift else face[i], part)
            packed.append(part)
        packed = jnp.concatenate(packed, 0)
        wide, row = lanes_of(ROWS), rows_of(ROWS)
        kind, receiver = wide // COUNT, wide % COUNT
        shift = jnp.where(kind == 2, 1, jnp.where(kind == 3, -1, 0))
        fits = ((kind < 2) & (row % 2 == kind)) | ((kind == 2) & (row == ROWS - 1)) | ((kind == 3) & (row == 0))
        picks, values = [], []
        for message, side in ((below, 0), (above, 1)):
            target = (place - neighbour_offsets(message, LANES) + shift + 2 * COUNT) & (COUNT - 1)
            picks.append(jnp.where(fits & (receiver == target), 1.0, 0.0))
            values.append(jnp.where((wide % 2 == side) & (wide < 18), packed, 0.0))
        sent = lax.dot_general(
            jnp.concatenate(picks, 0),
            jnp.concatenate(values, 0),
            (((0,), (0,)), ((), ())),
            precision=exact_mode,
            preferred_element_type=jnp.float32,
        )
        line = sent[0:COUNT]
        for k in range(1, 4):
            line = line + pltpu.roll(sent[COUNT * k : COUNT * (k + 1)], 32 * k, 1)
        for e in range(COUNT):
            slots[other + e, EDGE : EDGE + 1, :] = line[e : e + 1]


def finish_kernel(numbers, scales, post, strips, slots, below, above, out, halo, stand, ghost, mid, side, thin, stage, offsets, sems, small):
    fetch = pltpu.make_async_copy(numbers, offsets, small)
    fetch.start()
    group, place = group_and_place()
    own, other = COUNT * group, COUNT * (1 - group)
    lane = lanes_of(FRAME)

    def halos(annulus):
        for sense in (1, -1):
            slot = own + ((place - sense + COUNT) & (COUNT - 1))
            for n, (i, r, depth) in enumerate(halo_entries(annulus, sense)):
                row = 8 - depth if sense == 1 else depth - 1
                halo[i, r, 0, row : row + 1, :] = slots[slot, n : n + 1, :]
                line = CORNERS + n // 32
                turned = pltpu.roll(slots[slot, line : line + 1, :], (-4 * (n % 32) - 2) % LANES, 1)
                halo[i, r, 1, row : row + 1, :] = turned
            if annulus:
                for n in range(SUMS, SUMS + 6):
                    row = 7 if sense == 1 else 0
                    stand[n - SUMS, 0, row : row + 1, :] = slots[slot, n : n + 1, :]
                    line = CORNERS + n // 32
                    turned = pltpu.roll(slots[slot, line : line + 1, :], (-4 * (n % 32) - 2) % LANES, 1)
                    stand[n - SUMS, 1, row : row + 1, :] = turned

    @pl.when(group == 1)
    def _():
        halos(False)

    @pl.when(group == 0)
    def _():
        halos(True)

    fetch.wait()
    for q in range(COUNT):
        slot = other + partner(place, group, offsets[0, q])
        for i in range(9):
            ghost[i, 0, 2 * q : 2 * q + 2, :] = slots[slot, 2 * i : 2 * i + 2, :]

    def main_of(i, r):
        return jnp.concatenate([post[i, r], halo[i, r, 0]], 0)

    def strip_of(i, r):
        return jnp.concatenate([strips[i, r], halo[i, r, 1]], 0)

    def edged(main, column, cx):
        return jnp.where(lane == (0 if cx == 1 else LANES - 1), column, turned_by(main, cx, 1)) if cx else main

    def send(i):
        if i % 3 == 2:
            pltpu.make_async_copy(stage.at[pl.ds(i - 2, 3)], out.at[pl.ds(i - 2, 3)], sems.at[i // 3]).start()

    @pl.when(group == 1)
    def _():
        for i, (cr, ca, cx) in enumerate(speeds):
            for r in range(RADIAL):
                if r - cr == RADIAL:
                    stage[i, r] = ghost[i, 0, 0:ROWS]
                else:
                    source = (i - 18, 0) if r - cr == -1 else (i, r - cr)
                    main = edged(main_of(*source), turned_by(strip_of(*source), cx, 1) if cx else None, cx)
                    stage[i, r] = turned_by(main, ca, 0)[0:ROWS]
            send(i)

    @pl.when(group == 0)
    def _():
        before = other + ((place - 1 + offsets[0, COUNT - 1] + COUNT) & (COUNT - 1))
        after = other + ((place + 1 + offsets[0, 0] + COUNT) & (COUNT - 1))
        for i in range(9):
            ghost[i, 0, FRAME - 1 : FRAME, :] = slots[before, 18 + i : 19 + i, :]
            ghost[i, 0, ROWS : ROWS + 1, :] = slots[after, 27 + i : 28 + i, :]
        received = jnp.concatenate([slots[other + d, EDGE : EDGE + 1, :] for d in range(COUNT)], 0)
        stack = jnp.concatenate([received] + [pltpu.roll(received, LANES - 32 * k, 1) for k in range(1, 4)], 0)
        row, wide = rows_of(FRAME, 64), lax.broadcasted_iota(jnp.int32, (FRAME, 64), 1)
        kind, sender = wide // COUNT, wide % COUNT
        shift = jnp.where(kind == 2, -1, jnp.where(kind == 3, 1, 0))
        fits = ((kind < 2) & (row % 2 == kind) & (row < ROWS)) | ((kind == 2) & (row == FRAME - 1)) | ((kind == 3) & (row == ROWS))
        picked = []
        for message in (below, above):
            offset = neighbour_offsets(message, 64)
            tail = jnp.where(rows_of(8, 64) == 0, offset[0:1], offset[ROWS - 1 : ROWS])
            source = (place + jnp.concatenate([offset, tail], 0) + shift + COUNT) & (COUNT - 1)
            pick = jnp.where(fits & (sender == source), 1.0, 0.0)
            picked.append(
                lax.dot_general(
                    pick, stack, (((1,), (0,)), ((), ())), precision=exact_mode, preferred_element_type=jnp.float32
                )
            )
        columns = jnp.where(lane % 2 == 0, picked[0], picked[1])
        for i in range(9):
            ghost[i, 1] = turned_by(columns, LANES - 1 - 2 * i, 1)

        narrow, none = lanes_of(8), jnp.zeros((8, LANES), jnp.float32)
        for i, (cr, ca, cx) in enumerate(speeds):
            for r in range(RADIAL):
                if r - cr == -1:
                    main, strip = ghost[i - 18, 0], ghost[i - 18, 1]
                elif r - cr == RADIAL:
                    main, strip = main_of(26 - i, 1), strip_of(26 - i, 1)
                else:
                    main, strip = turned_by(main_of(i, r - cr), ca, 0), turned_by(strip_of(i, r - cr), ca, 0)
                    if cx:
                        near, far = turned_by(main, cx, 1), turned_by(strip, cx, 1)
                        edge = lane == (0 if cx == 1 else LANES - 1)
                        main, strip = jnp.where(edge, far, near), jnp.where(edge, near, far)
                if ca or r - cr == -1:
                    mid[i, r] = main
                    side[i, r] = strip
                else:
                    mid[i, r, 0:ROWS] = main[0:ROWS]
                    side[i, r, 0:ROWS] = strip[0:ROWS]
                    given = (i, r) in stand_ins
                    mid[i, r, ROWS:FRAME] = stand[stand_ins.index((i, r)), 0] if given else none
                    side[i, r, ROWS:FRAME] = stand[stand_ins.index((i, r)), 1] if given else none

        @pl.when(place >= 0)
        def _():
            for i in range(27):
                dense = jnp.zeros((8, LANES), jnp.float32)
                for r in range(RADIAL):
                    for g in range(5):
                        first = dense_lane(g, r)
                        dense = into(dense, side[i, r, 8 * g : 8 * g + 8, :], narrow, first, first + 2)
                thin[i] = dense

        def chunk(step, carry):
            r, rows = step // 5, pl.ds(pl.multiple_of(step % 5 * 8, 8), 8)
            g = [mid[i, r, rows, :] for i in range(27)]
            for i, value in enumerate(relax(g, [scales[k] for k in range(27)])):
                mid[i, r, rows, :] = value
            return carry

        lax.fori_loop(0, 10, chunk, 0)
        for i, value in enumerate(relax([thin[i] for i in range(27)], [scales[k] for k in range(27)])):
            thin[i] = value
        for i, (cr, ca, cx) in enumerate(speeds):
            for r in range(RADIAL):
                if r - cr == -1:
                    stage[i, r] = ghost[i - 18, 0, 0:ROWS]
                elif r - cr == RADIAL:
                    stage[i, r] = mid[26 - i, 1, 0:ROWS]
                else:
                    column = None
                    if cx:
                        dense, turn = thin[i], -1 if cx == 1 else LANES - 3
                        column = [turned_by(dense, turn - dense_lane(g, r - cr), 1) for g in range(5)]
                        column = jnp.concatenate(column, 0)
                    stage[i, r] = turned_by(edged(mid[i, r - cr], column, cx), ca, 0)[0:ROWS]
            send(i)

    for k in range(9):
        pltpu.make_async_copy(stage.at[pl.ds(3 * k, 3)], out.at[pl.ds(3 * k, 3)], sems.at[k]).wait()


def local(populations, relax_rates, tile_offsets):
    shape = functools.partial(jax.ShapeDtypeStruct, dtype=jnp.float32)
    block = (27, RADIAL, ROWS, LANES)
    params = pltpu.CompilerParams(vmem_limit_bytes=24 << 20)
    smem, vmem, hbm = [pl.BlockSpec(memory_space=m) for m in (pltpu.SMEM, pltpu.VMEM, pltpu.HBM)]
    columns = pl.pallas_call(
        number_kernel,
        out_shape=shape((8, LANES)),
        in_specs=[vmem],
        out_specs=vmem,
        compiler_params=params,
        cost_estimate=pl.CostEstimate(flops=500_000_000, bytes_accessed=4_000_000, transcendentals=0),
        name="number",
    )(tile_offsets)
    message = pl.pallas_call(
        pack_kernel,
        out_shape=shape((TILES, 8, LANES)),
        in_specs=[vmem, vmem],
        out_specs=vmem,
        compiler_params=params,
        name="pack",
    )(columns, populations[0])
    size = lax.axis_size("ax")
    up = [(i, (i + 1) % size) for i in range(size)]
    below = lax.ppermute(message, "ax", up)
    above = lax.ppermute(message, "ax", [(j, i) for i, j in up])
    post, slots, scales = pl.pallas_call(
        collide_kernel,
        out_shape=(shape(block), shape((2 * COUNT, SLOT_ROWS, LANES)), shape((28, 8, LANES))),
        in_specs=[smem, smem, vmem],
        out_specs=(vmem, vmem, vmem),
        scratch_shapes=[pltpu.VMEM((9, ROWS, LANES), jnp.float32)],
        compiler_params=params,
        cost_estimate=pl.CostEstimate(flops=80_000_000, bytes_accessed=1_800_000, transcendentals=0),
        name="collide",
    )(tile_offsets, relax_rates, populations[0])
    strips, slots = pl.pallas_call(
        edge_kernel,
        out_shape=(shape(block), shape((2 * COUNT, SLOT_ROWS, LANES))),
        in_specs=[vmem] * 5,
        out_specs=(vmem, vmem),
        scratch_shapes=[pltpu.VMEM((27, 8, LANES), jnp.float32), pltpu.VMEM((9, 8, LANES), jnp.float32)],
        compiler_params=params,
        name="edge",
    )(scales, post, below, above, slots)
    slots = lax.all_to_all(slots, ("grp", "az"), split_axis=0, concat_axis=0, tiled=True)
    out = pl.pallas_call(
        finish_kernel,
        out_shape=shape(block),
        in_specs=[hbm] + [vmem] * 6,
        out_specs=hbm,
        scratch_shapes=[
            pltpu.VMEM((27, RADIAL, 2, 8, LANES), jnp.float32),
            pltpu.VMEM((6, 2, 8, LANES), jnp.float32),
            pltpu.VMEM((9, 2, FRAME, LANES), jnp.float32),
            pltpu.VMEM((27, RADIAL, FRAME, LANES), jnp.float32),
            pltpu.VMEM((27, RADIAL, FRAME, LANES), jnp.float32),
            pltpu.VMEM((27, 8, LANES), jnp.float32),
            pltpu.VMEM(block, jnp.float32),
            pltpu.SMEM((1, COUNT), jnp.int32),
            pltpu.SemaphoreType.DMA((9,)),
            pltpu.SemaphoreType.DMA(()),
        ],
        compiler_params=params,
        name="finish",
    )(tile_offsets, scales, post, strips, slots, below, above)
    return out[None]


def solution(mesh):
    in_specs = (P("grp", None, None, "az", "ax"), P(), P("ax", None))
    out_specs = P("grp", None, None, "az", "ax")
    return jax.shard_map(local, mesh=mesh, in_specs=in_specs, out_specs=out_specs, check_vma=False)
```

```python
import functools

import jax
import jax.numpy as jnp
from jax import lax
from jax.experimental import pallas as pl
from jax.experimental.pallas import tpu as pltpu
from jax.sharding import PartitionSpec as P


RADIAL, ROWS, FRAME, LANES = 2, 32, 40, 128
COUNT, SLOTS = 16, 2
SLOT_ROWS = 40
SUMS = 30
CORNERS = 36
EDGE = 36
OFFSET_LANE = 96
TILES = 7
exact_mode = lax.Precision.HIGHEST
speeds = [(cr, ca, cx) for cr in (-1, 0, 1) for ca in (-1, 0, 1) for cx in (-1, 0, 1)]


def at(cr, ca, cx):
    return 9 * (cr + 1) + 3 * (ca + 1) + (cx + 1)


def moments(g):
    for stride in (1, 3, 9):
        out = [None] * 27
        for base in range(27):
            if base // stride % 3 == 0:
                low, mid, high = g[base], g[base + stride], g[base + 2 * stride]
                even = high + low
                out[base] = even + 4.0 * mid
                out[base + stride] = high - low
                out[base + 2 * stride] = even
        g = out
    return g


def balance_moments(m):
    third, ninth = 1.0 / 3.0, 1.0 / 9.0
    rho, jx, ja, jr = m[0], m[1], m[3], m[9]
    inverse = 1.0 / rho
    ur, ua, ux = jr * inverse, ja * inverse, jx * inverse
    rr, aa, xx = jr * ur, ja * ua, jx * ux
    rho3, rho9 = rho * third, rho * ninth
    jr3, ja3, jx3 = jr * third, ja * third, jx * third
    ra, rx, ax = jr * ua, jr * ux, ja * ux
    e = [None] * 27
    e[12], e[10], e[4] = ra, rx, ax
    e[18], e[6], e[2] = rho3 + rr, rho3 + aa, rho3 + xx
    e[21], e[19], e[15], e[11], e[5], e[7] = ja3, jx3, jr3, jr3, ja3, jx3
    e[22], e[16], e[14] = ax * third, rx * third, ra * third
    e[24], e[20], e[8] = rho9 + (rr + aa) * third, rho9 + (rr + xx) * third, rho9 + (aa + xx) * third
    e[25], e[23], e[17] = jx * ninth, ja * ninth, jr * ninth
    e[26] = rho * (1.0 / 27.0) + (rr + aa + xx) * ninth
    return e


def relax(g, rates):
    m = moments(g)
    e = balance_moments(m)
    d = [None] * 27
    for k in range(27):
        if k not in (0, 1, 3, 9):
            d[k] = (m[k] if e[k] is None else m[k] - e[k]) * rates[k]
    for stride in (1, 3, 9):
        out = [None] * 27
        for base in range(27):
            if base // stride % 3 == 0:
                low, mid, high = d[base], d[base + stride], d[base + 2 * stride]
                out[base] = high if mid is None else high - mid
                out[base + stride] = -0.5 * high if low is None else 0.5 * (low - high)
                out[base + 2 * stride] = high if mid is None else high + mid
        d = out
    return [g[i] - d[i] for i in range(27)]


def rescaled(before, after, group, factor):
    m = moments(before)
    rho = m[0] * (1.0 / 216.0)
    inverse = 1.0 / m[0]
    ur, ua, ux = m[9] * inverse, m[3] * inverse, m[1] * inverse
    rest = 1.0 - 1.5 * (ur * ur + ua * ua + ux * ux)
    outward = jnp.where(group == 0, -ur, ur)
    out = []
    for ca in (-1, 0, 1):
        for cx in (-1, 0, 1):
            along = outward
            along = along + ca * ua if ca else along
            along = along + cx * ux if cx else along
            e = rho * (rest + along * (3.0 + 4.5 * along))
            out.append(e + factor * (after[len(out)] - e))
    return out


def halo_entries(annulus, sense):
    out = []
    for depth in (1, 2) if annulus else (1,):
        for cx in (-1, 0, 1):
            out += [(at(0, sense, cx), 0, depth), (at(0, sense, cx), 1, depth)]
            out += [(at(1, sense, cx), 0, depth), (at(-1, sense, cx), 1, depth)]
    if annulus:
        out += [(at(1, ca, cx), 1, 1) for ca in (-1, 1) for cx in (-1, 0, 1)]
    else:
        out += [(at(-1, sense, cx), 0, 1) for cx in (-1, 0, 1)]
    return out


stand_ins = [(at(0, 0, 0), 0), (at(0, 0, 1), 0), (at(-1, 0, 0), 0), (at(0, 0, 0), 1), (at(0, 0, 1), 1), (at(1, 0, 0), 1)]


def stand_in_values(p0, q0, p1, r1, q1):
    quarter = 0.25
    along0 = (p0[2] - p0[0]) + quarter * (q0[2] - q0[0])
    still0 = p0[1] + quarter * (p0[2] + p0[0] - along0)
    inward0 = q0[1] + quarter * (q0[2] + q0[0])
    plus, minus = r1[1] + quarter * (r1[2] + r1[0]), q1[1] + quarter * (q1[2] + q1[0])
    along1 = (p1[2] - p1[0]) + quarter * ((r1[2] - r1[0]) + (q1[2] - q1[0]))
    still1 = p1[1] + quarter * (p1[2] + p1[0] - along1) + 0.5 * minus
    return [still0, along0, inward0, still1, along1, plus - minus]


def lanes_of(rows):
    return lax.broadcasted_iota(jnp.int32, (rows, LANES), 1)


def rows_of(rows, lanes=LANES):
    return lax.broadcasted_iota(jnp.int32, (rows, lanes), 0)


def group_and_place():
    return lax.axis_index("grp"), lax.axis_index("az")


def partner(place, group, offset):
    return (place + (1 - 2 * group) * offset + COUNT) & (COUNT - 1)


def dense_lane(group, r):
    return 4 * (2 * group + r)


def turned_by(tile, shift, axis):
    shift %= tile.shape[axis]
    return pltpu.roll(tile, shift, axis) if shift else tile


def into(acc, tile, lane, first, shift):
    turned = pltpu.roll(tile, shift % LANES, 1) if shift % LANES else tile
    return jnp.where(lane // 4 == first // 4, turned, acc)


def number_kernel(offsets, columns):
    lane = lanes_of(8)
    wide = lax.broadcasted_iota(jnp.int32, (8, COUNT), 1)
    line = jnp.broadcast_to(offsets[...].astype(jnp.float32), (8, COUNT))
    last = jnp.zeros((8, LANES), jnp.float32)
    for g in range(4):
        own = jnp.where(wide == 4 * g + rows_of(8, COUNT) // SLOTS, line, 0.0)
        last = jnp.where(lane == OFFSET_LANE + g, jnp.sum(own, axis=1, keepdims=True), last)
    columns[...] = last


def pack_kernel(columns, pops, message):
    lane = lanes_of(8)
    for i in range(27):
        if i % 4 == 0:
            acc = columns[...] if i == 24 else jnp.zeros((8, LANES), jnp.float32)
        for g in range(4):
            for r in range(RADIAL):
                first = 32 * (i % 4) + dense_lane(g, r)
                acc = into(acc, pops[i, r, 8 * g : 8 * g + 8, :], lane, first, first + 2)
        if i % 4 == 3 or i == 26:
            message[i // 4] = acc


def collide_kernel(numbers, rates, pops, post, slots, scales, face, offsets, small):
    fetch = pltpu.make_async_copy(numbers, offsets, small)
    fetch.start()
    group, place = group_and_place()
    own, other = COUNT * group, COUNT * (1 - group)
    mine = jnp.where(group == 0, rates[0:1, :], rates[1:2, :])
    for k in range(27):
        scales[k] = jnp.broadcast_to(mine[:, k : k + 1] * 0.125, (8, LANES))
    fine, coarse = rates[0:1, 12:13], rates[1:2, 12:13]
    factor = jnp.broadcast_to(jnp.where(group == 0, 2.0 * fine / coarse, coarse / (2.0 * fine)), (8, LANES))
    scales[27] = factor

    def chunk(step, carry):
        r, rows = step // 4, pl.ds(pl.multiple_of(step % 4 * 8, 8), 8)
        g = [pops[i, r, rows, :] for i in range(27)]
        for i, value in enumerate(relax(g, [scales[k] for k in range(27)])):
            post[i, r, rows, :] = value
        return carry

    lax.fori_loop(0, 8, chunk, 0)
    for g in range(4):
        rows = slice(8 * g, 8 * g + 8)
        before = [pops[i, group, rows, :] for i in range(27)]
        after = [post[18 * group + i, group, rows, :] for i in range(9)]
        for i, value in enumerate(rescaled(before, after, group, factor)):
            face[i, rows, :] = value

    def halos(annulus):
        for sense in (1, -1):
            slot = own + ((place + sense + COUNT) & (COUNT - 1))
            for n, (i, r, depth) in enumerate(halo_entries(annulus, sense)):
                row = ROWS - depth if sense == 1 else depth - 1
                slots[slot, n : n + 1, :] = post[i, r, row : row + 1, :]

    @pl.when(group == 0)
    def _():
        halos(True)

    @pl.when(group == 1)
    def _():
        halos(False)

    fetch.wait()
    for q in range(COUNT):
        slot = other + partner(place, group, offsets[0, q])
        for i in range(9):
            slots[slot, 2 * i : 2 * i + 2, :] = face[i, 2 * q : 2 * q + 2, :]
    after = other + ((place - offsets[0, COUNT - 1] + 1 + COUNT) & (COUNT - 1))
    before = other + ((place - offsets[0, 0] - 1 + COUNT) & (COUNT - 1))
    for i in range(9):
        slots[after, 18 + i : 19 + i, :] = face[i, ROWS - 1 : ROWS, :]
        slots[before, 27 + i : 28 + i, :] = face[i, 0:1, :]


def neighbour_offsets(message, width):
    lanes = [message[TILES - 1, :, OFFSET_LANE + g : OFFSET_LANE + g + 1] for g in range(4)]
    return jnp.concatenate([jnp.broadcast_to(x, (8, width)) for x in lanes], 0).astype(jnp.int32)


def halo_sums(post, strips, group):
    rows, lane = slice(8 * group, 8 * group + 8), lanes_of(8)

    def moved(cr, r):
        out = []
        for cx in (-1, 0, 1):
            main, strip = post[at(cr, 0, cx), r, rows, :], strips[at(cr, 0, cx), r, rows, :]
            if cx:
                near, far = turned_by(main, cx, 1), turned_by(strip, cx, 1)
                edge = lane == (0 if cx == 1 else LANES - 1)
                main, strip = jnp.where(edge, far, near), jnp.where(edge, near, far)
            out.append((main, strip))
        return out

    back = [(post[at(1, 0, -cx), 1, rows, :], strips[at(1, 0, -cx), 1, rows, :]) for cx in (-1, 0, 1)]
    parts = [moved(0, 0), moved(-1, 1), moved(0, 1), moved(1, 0), back]
    main, strip = [stand_in_values(*[[value[k] for value in part] for part in parts]) for k in (0, 1)]
    return list(zip(main, strip))


def edge_kernel(scales, post, below, above, given, strips, slots, dense, face):
    group, place = group_and_place()
    slots[...] = given[...]
    own, other = COUNT * group, COUNT * (1 - group)
    factor = scales[27]
    lane = lanes_of(8)
    merged = [jnp.where(lane % 4 < 2, below[k], above[k]) for k in range(TILES)]
    pops = [pltpu.roll(merged[i // 4], LANES - 32 * (i % 4), 1) if i % 4 else merged[i // 4] for i in range(27)]
    for i, value in enumerate(relax(pops, [scales[k] for k in range(27)])):
        dense[i] = value

    def halos(annulus):
        narrow = lax.broadcasted_iota(jnp.int32, (1, LANES), 1)
        for sense in (1, -1):
            slot = own + ((place + sense + COUNT) & (COUNT - 1))
            corners = [jnp.zeros((1, LANES), jnp.float32)] * 2
            for n, (i, r, depth) in enumerate(halo_entries(annulus, sense)):
                g, row = (3, 8 - depth) if sense == 1 else (0, depth - 1)
                shift = 4 * (n % 32) - dense_lane(g, r)
                corners[n // 32] = into(corners[n // 32], dense[i, row : row + 1, :], narrow, 4 * (n % 32), shift)
            if annulus:
                row = 7 if sense == 1 else 0
                for n, (main, strip) in enumerate(halo_sums(post, strips, 3 if sense == 1 else 0), SUMS):
                    slots[slot, n : n + 1, :] = main[row : row + 1]
                    shift = (4 * (n % 32) + 2) % LANES
                    corners[n // 32] = into(corners[n // 32], strip[row : row + 1], narrow, 4 * (n % 32), shift)
            for k in range(2):
                slots[slot, CORNERS + k : CORNERS + k + 1, :] = corners[k]

    for i in range(27):
        for r in range(RADIAL):
            for g in range(4):
                shift = LANES - dense_lane(g, r) - 2
                strips[i, r, 8 * g : 8 * g + 8, :] = pltpu.roll(dense[i], shift, 1)

    @pl.when(group == 0)
    def _():
        halos(True)

    @pl.when(group == 1)
    def _():
        halos(False)
        after = [dense[18 + i] for i in range(9)]
        for i, value in enumerate(rescaled(pops, after, group, factor)):
            face[i] = value
        packed = []
        for g in range(4):
            part = jnp.zeros((8, LANES), jnp.float32)
            for i in range(9):
                shift = (2 * i - dense_lane(g, 1) - 1) % LANES
                part = jnp.where(lane // 2 == i, pltpu.roll(face[i], shift, 1) if shift else face[i], part)
            packed.append(part)
        packed = jnp.concatenate(packed, 0)
        wide, row = lanes_of(ROWS), rows_of(ROWS)
        kind, receiver = wide // COUNT, wide % COUNT
        shift = jnp.where(kind == 2, 1, jnp.where(kind == 3, -1, 0))
        fits = ((kind < 2) & (row % 2 == kind)) | ((kind == 2) & (row == ROWS - 1)) | ((kind == 3) & (row == 0))
        picks, values = [], []
        for message, side in ((below, 0), (above, 1)):
            target = (place - neighbour_offsets(message, LANES) + shift + 2 * COUNT) & (COUNT - 1)
            picks.append(jnp.where(fits & (receiver == target), 1.0, 0.0))
            values.append(jnp.where((wide % 2 == side) & (wide < 18), packed, 0.0))
        sent = lax.dot_general(
            jnp.concatenate(picks, 0),
            jnp.concatenate(values, 0),
            (((0,), (0,)), ((), ())),
            precision=exact_mode,
            preferred_element_type=jnp.float32,
        )
        line = sent[0:COUNT]
        for k in range(1, 4):
            line = line + pltpu.roll(sent[COUNT * k : COUNT * (k + 1)], 32 * k, 1)
        for e in range(COUNT):
            slots[other + e, EDGE : EDGE + 1, :] = line[e : e + 1]


def finish_kernel(numbers, scales, post, strips, slots, below, above, out, halo, stand, ghost, mid, side, thin, stage, offsets, sems, small):
    fetch = pltpu.make_async_copy(numbers, offsets, small)
    fetch.start()
    group, place = group_and_place()
    own, other = COUNT * group, COUNT * (1 - group)
    lane = lanes_of(FRAME)

    def halos(annulus):
        for sense in (1, -1):
            slot = own + ((place - sense + COUNT) & (COUNT - 1))
            for n, (i, r, depth) in enumerate(halo_entries(annulus, sense)):
                row = 8 - depth if sense == 1 else depth - 1
                halo[i, r, 0, row : row + 1, :] = slots[slot, n : n + 1, :]
                line = CORNERS + n // 32
                turned = pltpu.roll(slots[slot, line : line + 1, :], (-4 * (n % 32) - 2) % LANES, 1)
                halo[i, r, 1, row : row + 1, :] = turned
            if annulus:
                for n in range(SUMS, SUMS + 6):
                    row = 7 if sense == 1 else 0
                    stand[n - SUMS, 0, row : row + 1, :] = slots[slot, n : n + 1, :]
                    line = CORNERS + n // 32
                    turned = pltpu.roll(slots[slot, line : line + 1, :], (-4 * (n % 32) - 2) % LANES, 1)
                    stand[n - SUMS, 1, row : row + 1, :] = turned

    @pl.when(group == 1)
    def _():
        halos(False)

    @pl.when(group == 0)
    def _():
        halos(True)

    fetch.wait()
    for q in range(COUNT):
        slot = other + partner(place, group, offsets[0, q])
        for i in range(9):
            ghost[i, 0, 2 * q : 2 * q + 2, :] = slots[slot, 2 * i : 2 * i + 2, :]

    def main_of(i, r):
        return jnp.concatenate([post[i, r], halo[i, r, 0]], 0)

    def strip_of(i, r):
        return jnp.concatenate([strips[i, r], halo[i, r, 1]], 0)

    def edged(main, column, cx):
        return jnp.where(lane == (0 if cx == 1 else LANES - 1), column, turned_by(main, cx, 1)) if cx else main

    def send(i):
        if i % 3 == 2:
            pltpu.make_async_copy(stage.at[pl.ds(i - 2, 3)], out.at[pl.ds(i - 2, 3)], sems.at[i // 3]).start()

    @pl.when(group == 1)
    def _():
        for i, (cr, ca, cx) in enumerate(speeds):
            for r in range(RADIAL):
                if r - cr == RADIAL:
                    stage[i, r] = ghost[i, 0, 0:ROWS]
                else:
                    source = (i - 18, 0) if r - cr == -1 else (i, r - cr)
                    main = edged(main_of(*source), turned_by(strip_of(*source), cx, 1) if cx else None, cx)
                    stage[i, r] = turned_by(main, ca, 0)[0:ROWS]
            send(i)

    @pl.when(group == 0)
    def _():
        before = other + ((place - 1 + offsets[0, COUNT - 1] + COUNT) & (COUNT - 1))
        after = other + ((place + 1 + offsets[0, 0] + COUNT) & (COUNT - 1))
        for i in range(9):
            ghost[i, 0, FRAME - 1 : FRAME, :] = slots[before, 18 + i : 19 + i, :]
            ghost[i, 0, ROWS : ROWS + 1, :] = slots[after, 27 + i : 28 + i, :]
        received = jnp.concatenate([slots[other + d, EDGE : EDGE + 1, :] for d in range(COUNT)], 0)
        stack = jnp.concatenate([received] + [pltpu.roll(received, LANES - 32 * k, 1) for k in range(1, 4)], 0)
        row, wide = rows_of(FRAME, 64), lax.broadcasted_iota(jnp.int32, (FRAME, 64), 1)
        kind, sender = wide // COUNT, wide % COUNT
        shift = jnp.where(kind == 2, -1, jnp.where(kind == 3, 1, 0))
        fits = ((kind < 2) & (row % 2 == kind) & (row < ROWS)) | ((kind == 2) & (row == FRAME - 1)) | ((kind == 3) & (row == ROWS))
        picked = []
        for message in (below, above):
            offset = neighbour_offsets(message, 64)
            tail = jnp.where(rows_of(8, 64) == 0, offset[0:1], offset[ROWS - 1 : ROWS])
            source = (place + jnp.concatenate([offset, tail], 0) + shift + COUNT) & (COUNT - 1)
            pick = jnp.where(fits & (sender == source), 1.0, 0.0)
            picked.append(
                lax.dot_general(
                    pick, stack, (((1,), (0,)), ((), ())), precision=exact_mode, preferred_element_type=jnp.float32
                )
            )
        columns = jnp.where(lane % 2 == 0, picked[0], picked[1])
        for i in range(9):
            ghost[i, 1] = turned_by(columns, LANES - 1 - 2 * i, 1)

        narrow, none = lanes_of(8), jnp.zeros((8, LANES), jnp.float32)
        for i, (cr, ca, cx) in enumerate(speeds):
            for r in range(RADIAL):
                if r - cr == -1:
                    main, strip = ghost[i - 18, 0], ghost[i - 18, 1]
                elif r - cr == RADIAL:
                    main, strip = main_of(26 - i, 1), strip_of(26 - i, 1)
                else:
                    main, strip = turned_by(main_of(i, r - cr), ca, 0), turned_by(strip_of(i, r - cr), ca, 0)
                    if cx:
                        near, far = turned_by(main, cx, 1), turned_by(strip, cx, 1)
                        edge = lane == (0 if cx == 1 else LANES - 1)
                        main, strip = jnp.where(edge, far, near), jnp.where(edge, near, far)
                if ca or r - cr == -1:
                    mid[i, r] = main
                    side[i, r] = strip
                else:
                    mid[i, r, 0:ROWS] = main[0:ROWS]
                    side[i, r, 0:ROWS] = strip[0:ROWS]
                    given = (i, r) in stand_ins
                    mid[i, r, ROWS:FRAME] = stand[stand_ins.index((i, r)), 0] if given else none
                    side[i, r, ROWS:FRAME] = stand[stand_ins.index((i, r)), 1] if given else none

        @pl.when(place >= 0)
        def _():
            for i in range(27):
                dense = jnp.zeros((8, LANES), jnp.float32)
                for r in range(RADIAL):
                    for g in range(5):
                        first = dense_lane(g, r)
                        dense = into(dense, side[i, r, 8 * g : 8 * g + 8, :], narrow, first, first + 2)
                thin[i] = dense

        def chunk(step, carry):
            r, rows = step // 5, pl.ds(pl.multiple_of(step % 5 * 8, 8), 8)
            g = [mid[i, r, rows, :] for i in range(27)]
            for i, value in enumerate(relax(g, [scales[k] for k in range(27)])):
                mid[i, r, rows, :] = value
            return carry

        lax.fori_loop(0, 10, chunk, 0)
        for i, value in enumerate(relax([thin[i] for i in range(27)], [scales[k] for k in range(27)])):
            thin[i] = value
        for i, (cr, ca, cx) in enumerate(speeds):
            for r in range(RADIAL):
                if r - cr == -1:
                    stage[i, r] = ghost[i - 18, 0, 0:ROWS]
                elif r - cr == RADIAL:
                    stage[i, r] = mid[26 - i, 1, 0:ROWS]
                else:
                    column = None
                    if cx:
                        dense, turn = thin[i], -1 if cx == 1 else LANES - 3
                        column = [turned_by(dense, turn - dense_lane(g, r - cr), 1) for g in range(5)]
                        column = jnp.concatenate(column, 0)
                    stage[i, r] = turned_by(edged(mid[i, r - cr], column, cx), ca, 0)[0:ROWS]
            send(i)

    for k in range(9):
        pltpu.make_async_copy(stage.at[pl.ds(3 * k, 3)], out.at[pl.ds(3 * k, 3)], sems.at[k]).wait()


def local(populations, relax_rates, tile_offsets):
    shape = functools.partial(jax.ShapeDtypeStruct, dtype=jnp.float32)
    block = (27, RADIAL, ROWS, LANES)
    params = pltpu.CompilerParams(vmem_limit_bytes=24 << 20)
    vmem, hbm = [pl.BlockSpec(memory_space=m) for m in (pltpu.VMEM, pltpu.HBM)]
    columns = pl.pallas_call(
        number_kernel,
        out_shape=shape((8, LANES)),
        in_specs=[vmem],
        out_specs=vmem,
        compiler_params=params,
        cost_estimate=pl.CostEstimate(flops=500_000_000, bytes_accessed=4_000_000, transcendentals=0),
        name="number",
    )(tile_offsets)
    message = pl.pallas_call(
        pack_kernel,
        out_shape=shape((TILES, 8, LANES)),
        in_specs=[vmem, vmem],
        out_specs=vmem,
        compiler_params=params,
        name="pack",
    )(columns, populations[0])
    size = lax.axis_size("ax")
    up = [(i, (i + 1) % size) for i in range(size)]
    below = lax.ppermute(message, "ax", up)
    above = lax.ppermute(message, "ax", [(j, i) for i, j in up])
    post, slots, scales = pl.pallas_call(
        collide_kernel,
        out_shape=(shape(block), shape((2 * COUNT, SLOT_ROWS, LANES)), shape((28, 8, LANES))),
        in_specs=[hbm, vmem, vmem],
        out_specs=(vmem, vmem, vmem),
        scratch_shapes=[
            pltpu.VMEM((9, ROWS, LANES), jnp.float32),
            pltpu.SMEM((1, COUNT), jnp.int32),
            pltpu.SemaphoreType.DMA(()),
        ],
        compiler_params=params,
        cost_estimate=pl.CostEstimate(flops=80_000_000, bytes_accessed=1_800_000, transcendentals=0),
        name="collide",
    )(tile_offsets, relax_rates, populations[0])
    strips, slots = pl.pallas_call(
        edge_kernel,
        out_shape=(shape(block), shape((2 * COUNT, SLOT_ROWS, LANES))),
        in_specs=[vmem] * 5,
        out_specs=(vmem, vmem),
        scratch_shapes=[pltpu.VMEM((27, 8, LANES), jnp.float32), pltpu.VMEM((9, 8, LANES), jnp.float32)],
        compiler_params=params,
        name="edge",
    )(scales, post, below, above, slots)
    slots = lax.all_to_all(slots, ("grp", "az"), split_axis=0, concat_axis=0, tiled=True)
    out = pl.pallas_call(
        finish_kernel,
        out_shape=shape(block),
        in_specs=[hbm] + [vmem] * 6,
        out_specs=hbm,
        scratch_shapes=[
            pltpu.VMEM((27, RADIAL, 2, 8, LANES), jnp.float32),
            pltpu.VMEM((6, 2, 8, LANES), jnp.float32),
            pltpu.VMEM((9, 2, FRAME, LANES), jnp.float32),
            pltpu.VMEM((27, RADIAL, FRAME, LANES), jnp.float32),
            pltpu.VMEM((27, RADIAL, FRAME, LANES), jnp.float32),
            pltpu.VMEM((27, 8, LANES), jnp.float32),
            pltpu.VMEM(block, jnp.float32),
            pltpu.SMEM((1, COUNT), jnp.int32),
            pltpu.SemaphoreType.DMA((9,)),
            pltpu.SemaphoreType.DMA(()),
        ],
        compiler_params=params,
        name="finish",
    )(tile_offsets, scales, post, strips, slots, below, above)
    return out[None]


def solution(mesh):
    in_specs = (P("grp", None, None, "az", "ax"), P(), P("ax", None))
    out_specs = P("grp", None, None, "az", "ax")
    return jax.shard_map(local, mesh=mesh, in_specs=in_specs, out_specs=out_specs, check_vma=False)
```
